32 devices in a mesh: modes: 16 (over z, x, core), gz: 2 (over y).
Axes of the slice: x: 2, y: 2, z: 4, core: 2. Of those that a mesh axis runs over, the one named last changes fastest.
Arguments:
- fields: float32 [288, 64, 4, 128], P('modes', None, 'gz'), may hold values from -6 to 6
- mean_coeff: float32 [64, 4, 128], P(None, 'gz'), may hold values from 0.5 to 4
- random_coeff: float32 [10, 64, 4, 128], P(None, None, 'gz'), may hold values from -2.5 to 2.5
- coupling: int32 [1606, 4], replicated, may hold values from 0 to 285, as said below
- mode_slots: int32 [286], replicated, may hold values from 0 to 287, as said below
Outputs:
- applied: float32 [288, 64, 4, 128], P('modes', None, 'gz')
The draws below stay inside these ranges and needn't reach their ends.
Inputs may be any that keep to these rules, and one draw needn't show every extreme that they name: `coupling`: each row couples a mode with itself under term 0, or a mode with the mode one higher in the degree of one variable under the term that belongs to that variable, in both orders; each of the 10 variables belongs to a different term of 1 to 10, in no particular assignment; every such pair appears exactly once, in no particular order; modes are numbered by total degree. `mode_slots`: the slots are distinct.
All inputs are finite; a program needn't handle non-finite values.
Results may differ from the reference program's by a relative error of at most 0.000082.
Values sent between devices are 32-bit elements; how exact they have to be, the bound alone decides.
A program may use at most 64 MiB of HBM per device.

```python
import math
import jax
import jax.numpy as jnp
import numpy as np
from jax import lax

NVAR = 10
CHAOS_MODES = 286
BAND_ROWS = 64
CELLS_ACROSS = 128
MODE_SLOT_TOTAL = 288
CELLS_DEPTH = 4


def chaos_table(count):
    indices = [[0] * count]
    for first_var in range(count):
        entry = [0] * count
        entry[first_var] += 1
        indices.append(entry)
    for first_var in range(count):
        for second_var in range(first_var, count):
            entry = [0] * count
            entry[first_var] += 1
            entry[second_var] += 1
            indices.append(entry)
    for first_var in range(count):
        for second_var in range(first_var, count):
            for third_var in range(second_var, count):
                entry = [0] * count
                entry[first_var] += 1
                entry[second_var] += 1
                entry[third_var] += 1
                indices.append(entry)
    lookup = {}
    for number, entry in enumerate(indices):
        lookup[tuple(entry)] = number
    row_list = [[number, number, 0, 0] for number in range(len(indices))]
    for number, entry in enumerate(indices):
        if sum(entry) < 3:
            for var_pos in range(count):
                raised = list(entry)
                raised[var_pos] += 1
                partner = lookup[tuple(raised)]
                row_list.append([number, partner, var_pos + 1, entry[var_pos]])
                row_list.append([partner, number, var_pos + 1, entry[var_pos]])
    return np.array(row_list, dtype=np.int32)


def draw_coupling(key, part):
    table = jnp.asarray(chaos_table(NVAR))
    term_key = jax.random.fold_in(key, 5)
    term_perm = jax.random.permutation(term_key, NVAR).astype(jnp.int32)
    old_terms = table[:, 2]
    safe_index = jnp.maximum(old_terms - 1, 0)
    new_terms = jnp.where(old_terms == 0, 0, term_perm[safe_index] + 1).astype(jnp.int32)
    table = jnp.stack([table[:, 0], table[:, 1], new_terms, table[:, 3]], axis=1)
    order = jax.random.permutation(key, table.shape[0])
    return table[order].astype(jnp.int32)


def draw_mode_slots(key, part):
    nested_key = jax.random.fold_in(key, 11)
    outer_key = jax.random.fold_in(key, 23)
    central_part = jax.random.permutation(nested_key, MODE_SLOT_TOTAL - 2).astype(jnp.int32)[:CHAOS_MODES - 2] + 1
    boundary_ends = jnp.array([0, MODE_SLOT_TOTAL - 1], dtype=jnp.int32)
    chosen = jnp.concatenate([boundary_ends, central_part])
    order = jax.random.permutation(outer_key, CHAOS_MODES)
    return chosen[order].astype(jnp.int32)


def level_of(key, extent, pieces, smallest, largest):
    def one(dim, parts):
        steps = jax.random.uniform(jax.random.fold_in(jax.random.fold_in(key, 6), dim), (parts,), jnp.float32, smallest / len(pieces), largest / len(pieces))
        return jnp.repeat(jnp.exp(steps), extent[dim] // parts).reshape((-1,) + (1,) * (len(extent) - dim - 1))

    loudness = one(*pieces[0])
    for cut in pieces[1:]:
        loudness = loudness * one(*cut)
    return loudness


def scatter_about(key, dims, scale, reach, cuts=(), kind=jnp.bfloat16):
    result = scale * jax.random.normal(key, dims, jnp.float32)
    if cuts:
        result = result * level_of(key, dims, cuts, -0.22, 0.18)
    return jnp.clip(result, -reach, reach).astype(kind)


def setup_inputs(seed: int = 0) -> dict:
    arg_keys = jax.random.split(jax.random.key(seed), 6)
    return {
        "fields": scatter_about(arg_keys[0], (MODE_SLOT_TOTAL, BAND_ROWS, CELLS_DEPTH, CELLS_ACROSS), 1.0, 6.0, ((0, 16), (2, 2)), jnp.float32),
        "mean_coeff": jnp.clip(jnp.exp(math.log(4.0) - 2.0794415 * jax.random.uniform(arg_keys[1], (BAND_ROWS, CELLS_DEPTH, CELLS_ACROSS), jnp.float32) ** level_of(arg_keys[1], (BAND_ROWS, CELLS_DEPTH, CELLS_ACROSS), ((1, 2),), -0.2, 0.2)), 0.5, 4.0),
        "random_coeff": scatter_about(arg_keys[2], (NVAR, BAND_ROWS, CELLS_DEPTH, CELLS_ACROSS), 0.4, 2.5, ((2, 2),), jnp.float32),
        "coupling": draw_coupling(jax.random.fold_in(arg_keys[5], 71), 0),
        "mode_slots": draw_mode_slots(jax.random.fold_in(arg_keys[5], 71), 0),
    }


def neighbour(values, axis_pos, offset):
    selector = [slice(None)] * values.ndim
    for position in range(values.ndim - 3, values.ndim):
        if position == axis_pos:
            selector[position] = slice(1 + offset, values.shape[position] - 1 + offset)
        else:
            selector[position] = slice(1, values.shape[position] - 1)
    return values[tuple(selector)]

def stencil_one(padded_field, padded_coef):
    value_here = neighbour(padded_field, 0, 0)
    coef_here = neighbour(padded_coef, 0, 0)
    summed = jnp.zeros(value_here.shape, jnp.float32)
    for axis_pos in range(3):
        for offset in (-1, 1):
            value_next = neighbour(padded_field, axis_pos, offset)
            coef_next = neighbour(padded_coef, axis_pos, offset)
            summed = summed + 0.5 * (coef_here + coef_next) * (value_here - value_next)
    return summed

def pair_weights(coupling):
    degree = coupling[:, 3].astype(jnp.float32)
    raw_weight = (degree + 1.0) / jnp.sqrt((2.0 * degree + 1.0) * (2.0 * degree + 3.0))
    return jnp.where(coupling[:, 2] == 0, jnp.ones_like(raw_weight), raw_weight)

def reference(fields, mean_coeff, random_coeff, coupling, mode_slots):
    coef = jnp.concatenate([mean_coeff[None], random_coeff], axis=0)
    weight = pair_weights(coupling)
    target = mode_slots[coupling[:, 0]].astype(jnp.int32)
    source = mode_slots[coupling[:, 1]].astype(jnp.int32)
    term_ids = coupling[:, 2].astype(jnp.int32)
    padding = ((0, 0), (1, 1), (1, 1), (1, 1))
    padded_fields = jnp.pad(fields, padding)
    padded_coef = jnp.pad(coef, padding)

    def accumulate(carry, entry):
        tgt_slot, src_slot, term_id, factor = entry
        source_field = lax.dynamic_index_in_dim(padded_fields, src_slot, 0, keepdims=False)
        term_coef = lax.dynamic_index_in_dim(padded_coef, term_id, 0, keepdims=False)
        image = stencil_one(source_field, term_coef)
        current = lax.dynamic_index_in_dim(carry, tgt_slot, 0, keepdims=False)
        carry = lax.dynamic_update_index_in_dim(carry, current + factor * image, tgt_slot, 0)
        return (carry, None)
    start = jnp.zeros(fields.shape, jnp.float32)
    applied, unused = lax.scan(accumulate, start, (target, source, term_ids, weight))
    return applied
```

```python
import functools

import jax
import jax.numpy as jnp
from jax import lax
from jax.experimental import pallas as pl
from jax.experimental.pallas import tpu as pltpu
from jax.sharding import PartitionSpec as P

CODE = 128
DEGREES = 3
MESH = pl.DeviceIdType.MESH


def rank_of(index, n):
    if n % 4:
        return index
    a, q = index // 4, lax.rem(index, 4)
    p = q + (q // 2) * (1 - 2 * lax.rem(q, 2))
    return a * 4 + p + lax.rem(a, 2) * (3 - 2 * p)


def index_of(rank, n):
    if n % 4:
        return rank
    a, p = rank // 4, lax.rem(rank, 4)
    p = p + lax.rem(a, 2) * (3 - 2 * p)
    return a * 4 + p + (p // 2) * (1 - 2 * lax.rem(p, 2))


def partner(me, step, n, sign):
    if n & (n - 1):
        return lax.rem(me + sign * step + n, n)
    bit = 1
    while bit < n:
        if step & bit:
            me = me + bit * (1 - 2 * lax.rem(me // bit, 2))
        bit *= 2
    return me


def step_order(n):
    near, far = list(range(1, n // 2)), list(range(n // 2, n))
    order = []
    while near or far:
        if far:
            order.append(far.pop(0))
        if near:
            order.append(near.pop(0))
    return order


def side_tiles(rows, depth):
    y_high = 0 if rows > 1 else 1
    z_low = y_high + 1
    z_high = z_low if depth > 1 else z_low + 1
    return (0, y_high, z_low, z_high), z_high + 1


def operator_kernel(n, g, rows, depth, modes, terms, slots, fields, mean, random, couple_in,
                    out, v, halo, dv, mixed, outs, couple, codes, coef, coef_halo, ctab, chalo,
                    cdiff, up_v, down_v, up, down, own_sem, send_sem, recv_sem, back_send,
                    back_recv, hsend, hrecv, csend, crecv, csem, tsem):
    me, layer = lax.axis_index("modes"), lax.axis_index("gz")
    own, lines = fields.shape[0], rows * depth
    lanes = fields.shape[3]
    rank = rank_of(me, n)
    before = index_of(lax.max(rank - 1, 0), n)
    after = index_of(lax.min(rank + 1, n - 1), n)
    tiles, tile_count = side_tiles(rows, depth)
    order = step_order(n)
    has = (rank > 0, rank < n - 1, layer > 0, layer < g - 1)
    to = ((before, layer), (after, layer), (me, layer - 1), (me, layer + 1))
    last = (rows - 1) * depth
    pieces = (
        [(0, depth, tiles[1], last)],
        [(last, depth, tiles[0], 0)],
        [(r * depth, 1, tiles[3], r * depth + depth - 1) for r in range(rows)],
        [(r * depth + depth - 1, 1, tiles[2], r * depth) for r in range(rows)],
    )
    source_side = (1, 0, 3, 2)

    barrier = pltpu.get_barrier_semaphore()

    @pl.loop(1, n)
    def _(step):
        pl.semaphore_signal(barrier, inc=1, device_id=(lax.rem(me + step, n), layer),
                            device_id_type=MESH)

    @pl.loop(1, g)
    def _(step):
        pl.semaphore_signal(barrier, inc=1, device_id=(me, lax.rem(layer + step, g)),
                            device_id_type=MESH)

    pl.semaphore_wait(barrier, n + g - 2)

    def block_copy(i):
        target = partner(me, order[i], n, 1)
        return pltpu.make_async_remote_copy(
            src_ref=fields.at[:, rank_of(target, n)], dst_ref=v.at[pl.ds(me * own, own)],
            send_sem=send_sem.at[i], recv_sem=recv_sem.at[i],
            device_id=(target, layer), device_id_type=MESH)

    def halo_copies(side, source):
        block = pl.ds(source * own, own)
        return [pltpu.make_async_remote_copy(
            src_ref=v.at[block, pl.ds(line, count)],
            dst_ref=halo.at[tile, block, pl.ds(land, count)],
            send_sem=hsend.at[side, source, j], recv_sem=hrecv.at[side, source, j],
            device_id=to[side], device_id_type=MESH)
            for j, (line, count, tile, land) in enumerate(pieces[side])]

    def coef_copies(side):
        copies = []
        for j, (line, count, tile, land) in enumerate(pieces[side]):
            for part, (src, dst) in enumerate((
                    (mean.at[:, rank, pl.ds(line, count)], coef_halo.at[tile, pl.ds(0, 1), pl.ds(land, count)]),
                    (random.at[:, rank, pl.ds(line, count)], coef_halo.at[tile, pl.ds(1, terms), pl.ds(land, count)]))):
                copies.append(pltpu.make_async_remote_copy(
                    src_ref=src, dst_ref=dst, send_sem=csend.at[side - 2, j, part],
                    recv_sem=crecv.at[side - 2, j, part], device_id=to[side], device_id_type=MESH))
        return copies

    for i in range(n - 1):
        block_copy(i).start()
    mine = pltpu.make_async_copy(fields.at[:, rank], v.at[pl.ds(me * own, own)], own_sem)
    mine.start()
    local = [
        pltpu.make_async_copy(couple_in, couple, csem.at[0]),
        pltpu.make_async_copy(mean.at[:, rank], coef.at[pl.ds(0, 1)], csem.at[1]),
        pltpu.make_async_copy(random.at[:, rank], coef.at[pl.ds(1, terms)], csem.at[2]),
    ]
    for copy in local:
        copy.start()

    def row_copies(side):
        line, count, tile, land = pieces[source_side[side]][0]
        there = lax.max(rank - 1, 0) if side == 0 else lax.min(rank + 1, n - 1)
        return [
            pltpu.make_async_copy(mean.at[:, there, pl.ds(line, count)],
                                  coef_halo.at[tile, pl.ds(0, 1), pl.ds(land, count)], csem.at[3 + side]),
            pltpu.make_async_copy(random.at[:, there, pl.ds(line, count)],
                                  coef_halo.at[tile, pl.ds(1, terms), pl.ds(land, count)], csem.at[5 + side])]

    for side in (0, 1):
        @pl.when(has[side])
        def _():
            for copy in row_copies(side):
                copy.start()
    for side in (2, 3):
        @pl.when(has[side])
        def _():
            for copy in coef_copies(side):
                copy.start()

    def send_halo(source):
        for side in range(4):
            @pl.when(has[side])
            def _():
                for copy in halo_copies(side, source):
                    copy.start()

    local[0].wait()
    sub = lax.broadcasted_iota(jnp.int32, (8, lanes), 0)
    lane8 = lax.broadcasted_iota(jnp.int32, (8, lanes), 1)
    pairs = couple.shape[1]
    highest = (n * own - 1) * CODE + terms * DEGREES
    source_mode = couple[1:2, :]

    def slot_block(b, total):
        first = b * 8
        mode = first + sub[:, :1]
        slot = jnp.zeros((8, 1), jnp.int32)
        for r in range(8):
            slot = jnp.where(sub[:, :1] == r, slots[jnp.minimum(first + r, modes - 1)], slot)
        return total + jnp.where(source_mode == mode, slot, 0)

    slot_of = lax.fori_loop(0, -(-modes // 8), slot_block, jnp.zeros((8, pairs), jnp.int32))
    slot_of = jnp.sum(slot_of, axis=0, keepdims=True)
    term = couple[2:3, :]
    index = jnp.where(term > 0, (term - 1) * DEGREES + couple[3:4, :] + 1, 0)
    codes[0:1, :] = slot_of * CODE + index
    codes[1:2, :] = jnp.where(term == 0, slot_of, -1)

    def block_of(b):
        return b * 8 + lax.broadcasted_iota(jnp.int32, (8, 1), 0)

    @pl.loop(0, up_v.shape[0] // 8)
    def _(b):
        mode = block_of(b)
        mask = (couple[0:1, :] == mode) & (couple[1:2, :] > mode)
        code = jnp.where(mask, codes[0:1, :], 0)
        table = jnp.zeros((8, lanes), jnp.int32)
        for k in range(terms):
            value = jnp.sum(jnp.where(couple[2:3, :] == k + 1, code, 0), axis=1, keepdims=True)
            table = jnp.where(lane8 == k, value, table)
        up_v[pl.ds(pl.multiple_of(b * 8, 8), 8), :] = jnp.clip(table, 0, highest)

    big = 2 ** 23

    @pl.loop(0, down_v.shape[0] // 8)
    def _(b):
        mode = block_of(b)
        code = codes[0:1, :]
        mask = (couple[0:1, :] == mode) & (couple[1:2, :] < mode)
        low = jnp.min(jnp.where(mask, code, big), axis=1, keepdims=True)
        high = jnp.max(jnp.where(mask, code, -1), axis=1, keepdims=True)
        total = jnp.sum(jnp.where(mask, code, 0), axis=1, keepdims=True)
        middle = jnp.maximum(total - low - high, 0)
        high = jnp.where(high > low, high, 0)
        low = jnp.where(low < big, low, 0)
        held = jnp.where(codes[1:2, :] == mode, couple[0:1, :] - modes, 0)
        held = jnp.clip(jnp.sum(held, axis=1, keepdims=True) + modes, 0, modes)
        table = jnp.zeros((8, lanes), jnp.int32)
        for k, value in enumerate((low, high, middle, held)):
            table = jnp.where(lane8 == k, value, table)
        down_v[pl.ds(pl.multiple_of(b * 8, 8), 8), :] = jnp.clip(table, 0, highest)

    moves = [pltpu.make_async_copy(up_v, up, tsem.at[0]), pltpu.make_async_copy(down_v, down, tsem.at[1])]
    for move in moves:
        move.start()

    line = lax.broadcasted_iota(jnp.int32, (1, lines, lanes), 1)
    lane = lax.broadcasted_iota(jnp.int32, (1, lines, lanes), 2)
    row, deep = line // depth, lax.rem(line, depth)
    side_masks = (
        (row == 0) & has[0], (row == rows - 1) & has[1],
        (deep == 0) & has[2], (deep == depth - 1) & has[3],
    )

    def differences(value, outside):
        total = 6.0 * value
        if rows > 1:
            total -= jnp.where(row == 0, 0.0, pltpu.roll(value, depth, 1))
            total -= jnp.where(row == rows - 1, 0.0, pltpu.roll(value, lines - depth, 1))
        if depth > 1:
            up_one, down_one = pltpu.roll(value, 1, 1), pltpu.roll(value, lines - 1, 1)
            if depth == 2:
                total -= jnp.where(deep == 0, down_one, up_one)
            else:
                total -= jnp.where(deep == 0, 0.0, up_one) + jnp.where(deep == depth - 1, 0.0, down_one)
        total -= jnp.where(lane == 0, 0.0, pltpu.roll(value, 1, 2))
        total -= jnp.where(lane == lanes - 1, 0.0, pltpu.roll(value, lanes - 1, 2))
        for tile in range(tile_count):
            mask = None
            for side in range(4):
                if tiles[side] == tile:
                    mask = side_masks[side] if mask is None else mask | side_masks[side]
            total -= jnp.where(mask, outside[tile], 0.0)
        return total

    for copy in local[1:]:
        copy.wait()
    for side in (0, 1):
        @pl.when(has[side])
        def _():
            for copy in row_copies(side):
                copy.wait()
    for side in (2, 3):
        @pl.when(has[side])
        def _():
            for copy in coef_copies(side):
                copy.wait_send()

        @pl.when(has[source_side[side]])
        def _():
            for copy in coef_copies(side):
                copy.wait_recv()

    here = coef[...]
    beyond = [coef_halo[tile] for tile in range(tile_count)]
    spread = differences(here, beyond)
    diagonal = terms * DEGREES + 1

    def put(place, k, weight):
        ctab[place] = weight * here[k]
        cdiff[place] = weight * spread[k]
        for tile in range(tile_count):
            chalo[tile, place] = weight * beyond[tile][k]

    zero = jnp.zeros((lines, lanes), jnp.float32)
    ctab[0] = zero
    cdiff[0] = zero
    for tile in range(tile_count):
        chalo[tile, 0] = zero
    for k in range(terms):
        for d in range(DEGREES):
            degree = jnp.full((1, 1), d, jnp.float32)
            weight = (degree + 1.0) * lax.rsqrt((2.0 * degree + 1.0) * (2.0 * degree + 3.0))
            put(k * DEGREES + d + 1, k + 1, 0.5 * weight)
    put(diagonal, 0, 0.5)

    mine.wait()
    send_halo(me)
    for i in range(n - 1):
        block_copy(i).wait_recv()
        send_halo(partner(me, order[i], n, -1))
    for i in range(n - 1):
        block_copy(i).wait_send()

    def finish_source(source):
        for side in range(4):
            @pl.when(has[source_side[side]])
            def _():
                for copy in halo_copies(side, source):
                    copy.wait_recv()
        block = pl.ds(source * own, own)
        dv[block] = differences(v[block], [halo[tile, block] for tile in range(tile_count)])

    finish_source(me)
    for i in range(n - 1):
        finish_source(partner(me, order[i], n, -1))
    for side in range(4):
        @pl.when(has[side])
        def _():
            @pl.loop(0, n)
            def _(source):
                for copy in halo_copies(side, source):
                    copy.wait_send()
    for move in moves:
        move.wait()

    def start(slot):
        value = v[slot]
        own_c = ctab[diagonal]
        total = [own_c * value, own_c * dv[slot] - cdiff[diagonal] * value]
        return total + [chalo[tile, diagonal] * halo[tile, slot] for tile in range(tile_count)]

    def add(total, code):
        slot, place = lax.shift_right_logical(code, 7), code & (CODE - 1)
        value, own_c = v[slot], ctab[place]
        new = [total[0] + own_c * value, total[1] + (own_c * dv[slot] - cdiff[place] * value)]
        return new + [total[2 + tile] + chalo[tile, place] * halo[tile, slot] for tile in range(tile_count)]

    def one_mode(i, ups, downs):
        total = start(slots[i])
        for k in range(ups):
            total = add(total, up[i, k])
        for k in range(downs):
            total = add(total, down[i, k])
        product = total[0][None]
        mixed[i] = (differences(product, [t[None] for t in total[2:]]) + total[1][None])[0]

    def level(first, stop, ups, downs, unroll):
        whole = (stop - first) // unroll

        @pl.loop(0, whole)
        def _(b):
            for u in range(unroll):
                one_mode(first + b * unroll + u, ups, downs)

        for i in range(first + whole * unroll, stop):
            one_mode(i, ups, downs)

    linear = 1 + terms
    square = linear + terms * (terms + 1) // 2
    level(0, 1, terms, 0, 1)
    level(1, linear, terms, 1, 2)
    level(linear, square, terms, 2, 5)
    level(square, modes, 0, 3, 10)
    mixed[modes] = zero

    def back_copy(i):
        target = partner(me, order[i], n, 1)
        return pltpu.make_async_remote_copy(
            src_ref=outs.at[pl.ds(target * own, own)], dst_ref=out.at[:, rank],
            send_sem=back_send.at[i], recv_sem=back_recv.at[i],
            device_id=(target, layer), device_id_type=MESH)

    def gather(target):
        for j in range(own):
            outs[target * own + j] = mixed[down[target * own + j, 3]]

    for i in range(n - 1):
        gather(partner(me, order[i], n, 1))
        back_copy(i).start()
    gather(me)
    mine = pltpu.make_async_copy(outs.at[pl.ds(me * own, own)], out.at[:, rank], own_sem)
    mine.start()
    mine.wait()
    for i in range(n - 1):
        pltpu.make_async_remote_copy(
            src_ref=outs.at[pl.ds(me * own, own)],
            dst_ref=out.at[:, rank_of(partner(me, order[i], n, -1), n)],
            send_sem=back_send.at[i], recv_sem=back_recv.at[i],
            device_id=(partner(me, order[i], n, 1), layer), device_id_type=MESH).wait_recv()
    for i in range(n - 1):
        back_copy(i).wait_send()


def store_kernel(source, out, held, into, back):
    count = source.shape[0]
    for i in range(count):
        pltpu.make_async_copy(source.at[i], held.at[i], into.at[i]).start()
    for i in range(count):
        pltpu.make_async_copy(source.at[i], held.at[i], into.at[i]).wait()
        pltpu.make_async_copy(held.at[i], out.at[i], back.at[i]).start()
    for i in range(count):
        pltpu.make_async_copy(held.at[i], out.at[i], back.at[i]).wait()


def body(fields, mean_coeff, random_coeff, coupling, mode_slots):
    n, g = lax.axis_size("modes"), lax.axis_size("gz")
    own, row_total, depth, across = fields.shape
    rows = row_total // n
    lines = rows * depth
    terms = random_coeff.shape[0]
    modes, pairs = mode_slots.shape[0], coupling.shape[0]
    f32, i32 = jnp.float32, jnp.int32
    smem = pl.BlockSpec(memory_space=pltpu.SMEM)
    anywhere = pl.BlockSpec(memory_space=pl.ANY)
    dma = pltpu.SemaphoreType.DMA
    _, tile_count = side_tiles(rows, depth)
    places = terms * DEGREES + 2
    low_modes = 1 + terms + terms * (terms + 1) // 2
    up_rows = -(-low_modes // 8) * 8
    down_rows = -(-max(modes, n * own) // 8) * 8

    def tile(*lead):
        return pltpu.VMEM((*lead, lines, across), f32)

    local = (own, n, lines, across)
    operator = pl.pallas_call(
        functools.partial(operator_kernel, n, g, rows, depth, modes, terms),
        out_shape=jax.ShapeDtypeStruct(local, f32),
        in_specs=[smem] + [anywhere] * 4,
        out_specs=anywhere,
        scratch_shapes=[
            tile(n * own), tile(tile_count, n * own), tile(n * own), tile(modes + 1), tile(n * own),
            pltpu.VMEM((4, pairs), i32), pltpu.VMEM((2, pairs), i32),
            tile(terms + 1), tile(tile_count, terms + 1),
            tile(places), tile(tile_count, places), tile(places),
            pltpu.VMEM((up_rows, across), i32), pltpu.VMEM((down_rows, across), i32),
            pltpu.SMEM((up_rows, across), i32), pltpu.SMEM((down_rows, across), i32),
            dma, dma((n - 1,)), dma((n - 1,)), dma((n - 1,)), dma((n - 1,)),
            dma((4, n, rows)), dma((4, n, rows)), dma((2, rows, 2)), dma((2, rows, 2)),
            dma((7,)), dma((2,)),
        ],
        compiler_params=pltpu.CompilerParams(collective_id=0, has_side_effects=True),
        name="operator",
    )
    result = operator(
        mode_slots, fields.reshape(local), mean_coeff.reshape(1, n, lines, across),
        random_coeff.reshape(terms, n, lines, across), coupling.T)

    store = pl.pallas_call(
        store_kernel,
        out_shape=jax.ShapeDtypeStruct(local, f32),
        in_specs=[anywhere],
        out_specs=anywhere,
        scratch_shapes=[pltpu.VMEM(local, f32), dma((own,)), dma((own,))],
        name="store",
    )
    return store(result).reshape(fields.shape)


def solution(mesh):
    in_specs = (
        P("modes", None, "gz", None),
        P(None, "gz", None),
        P(None, None, "gz", None),
        P(),
        P(),
    )
    out_specs = P("modes", None, "gz", None)
    return jax.shard_map(body, mesh=mesh, in_specs=in_specs, out_specs=out_specs, check_vma=False)
```

```python
import functools

import jax
import jax.numpy as jnp
from jax import lax
from jax.experimental import pallas as pl
from jax.experimental.pallas import tpu as pltpu
from jax.sharding import PartitionSpec as P

CODE = 128
DEGREES = 3
UNROLL_LOW = 5
UNROLL_HIGH = 9
MESH = pl.DeviceIdType.MESH


def rank_of(index, n):
    if n % 4:
        return index
    a, q = index // 4, lax.rem(index, 4)
    p = q + (q // 2) * (1 - 2 * lax.rem(q, 2))
    return a * 4 + p + lax.rem(a, 2) * (3 - 2 * p)


def index_of(rank, n):
    if n % 4:
        return rank
    a, p = rank // 4, lax.rem(rank, 4)
    p = p + lax.rem(a, 2) * (3 - 2 * p)
    return a * 4 + p + (p // 2) * (1 - 2 * lax.rem(p, 2))


def partner(me, step, n, sign):
    if n & (n - 1):
        return lax.rem(me + sign * step + n, n)
    bit = 1
    while bit < n:
        if step & bit:
            me = me + bit * (1 - 2 * lax.rem(me // bit, 2))
        bit *= 2
    return me


def step_order(n):
    near, far = list(range(1, n // 2)), list(range(n // 2, n))
    order = []
    while near or far:
        if far:
            order.append(far.pop(0))
        if near:
            order.append(near.pop(0))
    return order


def side_tiles(rows, depth):
    y_high = 0 if rows > 1 else 1
    z_low = y_high + 1
    z_high = z_low if depth > 1 else z_low + 1
    return (0, y_high, z_low, z_high), z_high + 1


def operator_kernel(n, g, rows, depth, modes, terms, slots, fields, mean, random, couple_in,
                    out, held, low_out, outs, couple, codes, coef, coef_halo, ctab,
                    up_v, down_v, high_v, up, down, high, own_sem, send_sem, recv_sem, back_send,
                    back_recv, hsend, hrecv, csend, crecv, csem, tsem):
    me, layer = lax.axis_index("modes"), lax.axis_index("gz")
    own, lines = fields.shape[0], rows * depth
    lanes = fields.shape[3]
    rank = rank_of(me, n)
    before = index_of(lax.max(rank - 1, 0), n)
    after = index_of(lax.min(rank + 1, n - 1), n)
    tiles, tile_count = side_tiles(rows, depth)
    order = step_order(n)
    has = (rank > 0, rank < n - 1, layer > 0, layer < g - 1)
    to = ((before, layer), (after, layer), (me, layer - 1), (me, layer + 1))
    last = (rows - 1) * depth
    pieces = (
        [(0, depth, tiles[1], last)],
        [(last, depth, tiles[0], 0)],
        [(r * depth, 1, tiles[3], r * depth + depth - 1) for r in range(rows)],
        [(r * depth + depth - 1, 1, tiles[2], r * depth) for r in range(rows)],
    )
    source_side = (1, 0, 3, 2)

    barrier = pltpu.get_barrier_semaphore()

    @pl.loop(1, n)
    def _(step):
        pl.semaphore_signal(barrier, inc=1, device_id=(lax.rem(me + step, n), layer),
                            device_id_type=MESH)

    @pl.loop(1, g)
    def _(step):
        pl.semaphore_signal(barrier, inc=1, device_id=(me, lax.rem(layer + step, g)),
                            device_id_type=MESH)

    pl.semaphore_wait(barrier, n + g - 2)

    def block_copy(i):
        target = partner(me, order[i], n, 1)
        return pltpu.make_async_remote_copy(
            src_ref=fields.at[:, rank_of(target, n)], dst_ref=held.at[pl.ds(me * own, own), 0],
            send_sem=send_sem.at[i], recv_sem=recv_sem.at[i],
            device_id=(target, layer), device_id_type=MESH)

    def halo_copies(side, source):
        block = pl.ds(source * own, own)
        return [pltpu.make_async_remote_copy(
            src_ref=held.at[block, 0, pl.ds(line, count)],
            dst_ref=held.at[block, 1 + tile, pl.ds(land, count)],
            send_sem=hsend.at[side, source, j], recv_sem=hrecv.at[side, source, j],
            device_id=to[side], device_id_type=MESH)
            for j, (line, count, tile, land) in enumerate(pieces[side])]

    def coef_copies(side):
        copies = []
        for j, (line, count, tile, land) in enumerate(pieces[side]):
            for part, (src, dst) in enumerate((
                    (mean.at[:, rank, pl.ds(line, count)], coef_halo.at[tile, pl.ds(0, 1), pl.ds(land, count)]),
                    (random.at[:, rank, pl.ds(line, count)], coef_halo.at[tile, pl.ds(1, terms), pl.ds(land, count)]))):
                copies.append(pltpu.make_async_remote_copy(
                    src_ref=src, dst_ref=dst, send_sem=csend.at[side - 2, j, part],
                    recv_sem=crecv.at[side - 2, j, part], device_id=to[side], device_id_type=MESH))
        return copies

    for i in range(n - 1):
        block_copy(i).start()
    mine = pltpu.make_async_copy(fields.at[:, rank], held.at[pl.ds(me * own, own), 0], own_sem)
    mine.start()
    local = [
        pltpu.make_async_copy(couple_in, couple, csem.at[0]),
        pltpu.make_async_copy(mean.at[:, rank], coef.at[pl.ds(0, 1)], csem.at[1]),
        pltpu.make_async_copy(random.at[:, rank], coef.at[pl.ds(1, terms)], csem.at[2]),
    ]
    for copy in local:
        copy.start()

    def row_copies(side):
        line, count, tile, land = pieces[source_side[side]][0]
        there = lax.max(rank - 1, 0) if side == 0 else lax.min(rank + 1, n - 1)
        return [
            pltpu.make_async_copy(mean.at[:, there, pl.ds(line, count)],
                                  coef_halo.at[tile, pl.ds(0, 1), pl.ds(land, count)], csem.at[3 + side]),
            pltpu.make_async_copy(random.at[:, there, pl.ds(line, count)],
                                  coef_halo.at[tile, pl.ds(1, terms), pl.ds(land, count)], csem.at[5 + side])]

    for side in (0, 1):
        @pl.when(has[side])
        def _():
            for copy in row_copies(side):
                copy.start()
    for side in (2, 3):
        @pl.when(has[side])
        def _():
            for copy in coef_copies(side):
                copy.start()

    def send_halo(source):
        for side in range(4):
            @pl.when(has[side])
            def _():
                for copy in halo_copies(side, source):
                    copy.start()

    local[0].wait()
    sub = lax.broadcasted_iota(jnp.int32, (8, lanes), 0)
    lane8 = lax.broadcasted_iota(jnp.int32, (8, lanes), 1)
    pairs = couple.shape[1]
    highest = (n * own - 1) * CODE + terms * DEGREES
    linear = 1 + terms
    square = linear + terms * (terms + 1) // 2

    def slot_block(b, total):
        mode = b * 8 + sub[:, :1]
        slot = jnp.zeros((8, 1), jnp.int32)
        for r in range(8):
            slot = jnp.where(sub[:, :1] == r, slots[jnp.minimum(b * 8 + r, modes - 1)], slot)
        return tuple(t + jnp.where(couple[j:j + 1, :] == mode, slot, 0) for j, t in enumerate(total))

    zeros = jnp.zeros((8, pairs), jnp.int32)
    found = lax.fori_loop(0, -(-modes // 8), slot_block, (zeros, zeros))
    target_slot, source_slot = (jnp.sum(f, axis=0, keepdims=True) for f in found)
    term = couple[2:3, :]
    index = jnp.where(term > 0, (term - 1) * DEGREES + couple[3:4, :] + 1, 0)
    codes[0:1, :] = source_slot * CODE + index
    codes[1:2, :] = target_slot

    def block_of(b):
        return b * 8 + lax.broadcasted_iota(jnp.int32, (8, 1), 0)

    def write(ref, b, values):
        table = jnp.zeros((8, lanes), jnp.int32)
        for k, value in enumerate(values):
            table = jnp.where(lane8 == k, value, table)
        ref[pl.ds(pl.multiple_of(b * 8, 8), 8), :] = jnp.clip(table, 0, highest)

    def lower(mask):
        code, big = codes[0:1, :], 2 ** 23
        mask = mask & (couple[1:2, :] < couple[0:1, :])
        low = jnp.min(jnp.where(mask, code, big), axis=1, keepdims=True)
        high = jnp.max(jnp.where(mask, code, -1), axis=1, keepdims=True)
        total = jnp.sum(jnp.where(mask, code, 0), axis=1, keepdims=True)
        middle = jnp.maximum(total - low - high, 0)
        return [jnp.where(low < big, low, 0), jnp.where(high > low, high, 0), middle]

    @pl.loop(0, up_v.shape[0] // 8)
    def _(b):
        here = couple[0:1, :] == block_of(b)
        code = jnp.where(here & (couple[1:2, :] > couple[0:1, :]), codes[0:1, :], 0)
        write(up_v, b, [jnp.sum(jnp.where(couple[2:3, :] == k + 1, code, 0), axis=1, keepdims=True)
                        for k in range(terms)])
        write(down_v, b, lower(here))

    @pl.loop(0, high_v.shape[0] // 8)
    def _(b):
        here = codes[1:2, :] == block_of(b)
        mode = jnp.where(here & (couple[2:3, :] == 0), couple[0:1, :] - modes, 0)
        mode = jnp.sum(mode, axis=1, keepdims=True) + modes
        is_high = (mode >= square) & (mode < modes)
        write(high_v, b, lower(here) + [jnp.clip(mode, 0, square), jnp.where(is_high, 1, 0)])

    moves = [pltpu.make_async_copy(a, b, tsem.at[i])
             for i, (a, b) in enumerate(((up_v, up), (down_v, down), (high_v, high)))]
    for move in moves:
        move.start()

    line = lax.broadcasted_iota(jnp.int32, (1, lines, lanes), 1)
    lane = lax.broadcasted_iota(jnp.int32, (1, lines, lanes), 2)
    row, deep = line // depth, lax.rem(line, depth)
    side_masks = (
        (row == 0) & has[0], (row == rows - 1) & has[1],
        (deep == 0) & has[2], (deep == depth - 1) & has[3],
    )

    def differences(value, outside):
        total = 6.0 * value
        if rows > 1:
            total -= jnp.where(row == 0, 0.0, pltpu.roll(value, depth, 1))
            total -= jnp.where(row == rows - 1, 0.0, pltpu.roll(value, lines - depth, 1))
        if depth > 1:
            up_one, down_one = pltpu.roll(value, 1, 1), pltpu.roll(value, lines - 1, 1)
            if depth == 2:
                total -= jnp.where(deep == 0, down_one, up_one)
            else:
                total -= jnp.where(deep == 0, 0.0, up_one) + jnp.where(deep == depth - 1, 0.0, down_one)
        total -= jnp.where(lane == 0, 0.0, pltpu.roll(value, 1, 2))
        total -= jnp.where(lane == lanes - 1, 0.0, pltpu.roll(value, lanes - 1, 2))
        for tile in range(tile_count):
            mask = None
            for side in range(4):
                if tiles[side] == tile:
                    mask = side_masks[side] if mask is None else mask | side_masks[side]
            total -= jnp.where(mask, outside[tile], 0.0)
        return total

    for copy in local[1:]:
        copy.wait()
    for side in (0, 1):
        @pl.when(has[side])
        def _():
            for copy in row_copies(side):
                copy.wait()
    for side in (2, 3):
        @pl.when(has[side])
        def _():
            for copy in coef_copies(side):
                copy.wait_send()

        @pl.when(has[source_side[side]])
        def _():
            for copy in coef_copies(side):
                copy.wait_recv()

    here = coef[...]
    beyond = [coef_halo[tile] for tile in range(tile_count)]
    spread = differences(here, beyond)
    diagonal = terms * DEGREES + 1

    def put(place, k, weight):
        for j, value in enumerate((here, *beyond, spread)):
            ctab[place, j] = weight * value[k]

    zero = jnp.zeros((lines, lanes), jnp.float32)
    for j in range(tile_count + 2):
        ctab[0, j] = zero
    for k in range(terms):
        for d in range(DEGREES):
            degree = jnp.full((1, 1), d, jnp.float32)
            weight = (degree + 1.0) * lax.rsqrt((2.0 * degree + 1.0) * (2.0 * degree + 3.0))
            put(k * DEGREES + d + 1, k + 1, 0.5 * weight)
    put(diagonal, 0, 0.5)

    mine.wait()
    send_halo(me)
    for i in range(n - 1):
        block_copy(i).wait_recv()
        send_halo(partner(me, order[i], n, -1))
    for i in range(n - 1):
        block_copy(i).wait_send()

    def finish_source(source):
        for side in range(4):
            @pl.when(has[source_side[side]])
            def _():
                for copy in halo_copies(side, source):
                    copy.wait_recv()
        block = pl.ds(source * own, own)
        held[block, tile_count + 1] = differences(
            held[block, 0], [held[block, 1 + tile] for tile in range(tile_count)])

    finish_source(me)
    for i in range(n - 1):
        finish_source(partner(me, order[i], n, -1))
    for side in range(4):
        @pl.when(has[side])
        def _():
            @pl.loop(0, n)
            def _(source):
                for copy in halo_copies(side, source):
                    copy.wait_send()
    for move in moves:
        move.wait()

    def add(total, slot, place):
        value, spread = held[slot, 0], held[slot, tile_count + 1]
        c, c_spread = ctab[place, 0], ctab[place, tile_count + 1]
        new = [c * value, c * spread - c_spread * value]
        new += [ctab[place, 1 + tile] * held[slot, 1 + tile] for tile in range(tile_count)]
        return new if total is None else [a + b for a, b in zip(total, new)]

    def add_code(total, code):
        return add(total, lax.shift_right_logical(code, 7), code & (CODE - 1))

    def finish(totals):
        product, other, *outside = (jnp.stack(part) for part in zip(*totals))
        return differences(product, outside) + other

    def low_modes(first, count, ups, downs):
        totals = []
        for u in range(count):
            total = add(None, slots[first + u], diagonal)
            for k in range(ups):
                total = add_code(total, up[first + u, k])
            for k in range(downs):
                total = add_code(total, down[first + u, k])
            totals.append(total)
        result = finish(totals)
        for u in range(count):
            low_out[first + u] = result[u]

    def level(first, stop, downs, unroll):
        whole = (stop - first) // unroll

        @pl.loop(0, whole)
        def _(b):
            low_modes(first + b * unroll, unroll, terms, downs)

        if first + whole * unroll < stop:
            low_modes(first + whole * unroll, stop - first - whole * unroll, terms, downs)

    level(0, 1, 0, 1)
    level(1, linear, 1, UNROLL_LOW)
    level(linear, square, 2, UNROLL_LOW)
    low_out[square] = zero

    def slot_group(first, count):
        totals = []
        for u in range(count):
            total = add(None, first + u, diagonal)
            for k in range(DEGREES):
                total = add_code(total, high[first + u, k])
            totals.append(total)
        result = finish(totals)
        result = [jnp.where(high[first + u, 4] > 0, result[u], low_out[high[first + u, 3]])
                  for u in range(count)]
        for u in range(count):
            outs[first + u] = result[u]

    def owner(target):
        unroll = max(u for u in range(1, UNROLL_HIGH + 1) if own % u == 0)

        @pl.loop(0, own // unroll)
        def _(b):
            slot_group(target * own + b * unroll, unroll)

    def back_copy(i):
        target = partner(me, order[i], n, 1)
        return pltpu.make_async_remote_copy(
            src_ref=outs.at[pl.ds(target * own, own)], dst_ref=out.at[:, rank],
            send_sem=back_send.at[i], recv_sem=back_recv.at[i],
            device_id=(target, layer), device_id_type=MESH)

    for i in range(n - 1):
        owner(partner(me, order[i], n, 1))
        back_copy(i).start()
    owner(me)
    mine = pltpu.make_async_copy(outs.at[pl.ds(me * own, own)], out.at[:, rank], own_sem)
    mine.start()
    mine.wait()
    for i in range(n - 1):
        pltpu.make_async_remote_copy(
            src_ref=outs.at[pl.ds(me * own, own)],
            dst_ref=out.at[:, rank_of(partner(me, order[i], n, -1), n)],
            send_sem=back_send.at[i], recv_sem=back_recv.at[i],
            device_id=(partner(me, order[i], n, 1), layer), device_id_type=MESH).wait_recv()
    for i in range(n - 1):
        back_copy(i).wait_send()


def store_kernel(source, out, held, into, back):
    count = source.shape[0]
    for i in range(count):
        pltpu.make_async_copy(source.at[i], held.at[i], into.at[i]).start()
    for i in range(count):
        pltpu.make_async_copy(source.at[i], held.at[i], into.at[i]).wait()
        pltpu.make_async_copy(held.at[i], out.at[i], back.at[i]).start()
    for i in range(count):
        pltpu.make_async_copy(held.at[i], out.at[i], back.at[i]).wait()


def body(fields, mean_coeff, random_coeff, coupling, mode_slots):
    n, g = lax.axis_size("modes"), lax.axis_size("gz")
    own, row_total, depth, across = fields.shape
    rows = row_total // n
    lines = rows * depth
    terms = random_coeff.shape[0]
    modes, pairs = mode_slots.shape[0], coupling.shape[0]
    f32, i32 = jnp.float32, jnp.int32
    smem = pl.BlockSpec(memory_space=pltpu.SMEM)
    anywhere = pl.BlockSpec(memory_space=pl.ANY)
    dma = pltpu.SemaphoreType.DMA
    _, tile_count = side_tiles(rows, depth)
    places = terms * DEGREES + 2
    low_modes = 1 + terms + terms * (terms + 1) // 2
    low_rows = -(-low_modes // 8) * 8
    slot_rows = -(-n * own // 8) * 8

    def tile(*lead):
        return pltpu.VMEM((*lead, lines, across), f32)

    local = (own, n, lines, across)
    operator = pl.pallas_call(
        functools.partial(operator_kernel, n, g, rows, depth, modes, terms),
        out_shape=jax.ShapeDtypeStruct(local, f32),
        in_specs=[smem] + [anywhere] * 4,
        out_specs=anywhere,
        scratch_shapes=[
            tile(n * own, tile_count + 2), tile(low_modes + 1), tile(n * own),
            pltpu.VMEM((4, pairs), i32), pltpu.VMEM((2, pairs), i32),
            tile(terms + 1), tile(tile_count, terms + 1), tile(places, tile_count + 2),
            *(pltpu.VMEM((size, across), i32) for size in (low_rows, low_rows, slot_rows)),
            *(pltpu.SMEM((size, across), i32) for size in (low_rows, low_rows, slot_rows)),
            dma, dma((n - 1,)), dma((n - 1,)), dma((n - 1,)), dma((n - 1,)),
            dma((4, n, rows)), dma((4, n, rows)), dma((2, rows, 2)), dma((2, rows, 2)),
            dma((7,)), dma((3,)),
        ],
        compiler_params=pltpu.CompilerParams(collective_id=0, has_side_effects=True),
        name="operator",
    )
    result = operator(
        mode_slots, fields.reshape(local), mean_coeff.reshape(1, n, lines, across),
        random_coeff.reshape(terms, n, lines, across), coupling.T)

    store = pl.pallas_call(
        store_kernel,
        out_shape=jax.ShapeDtypeStruct(local, f32),
        in_specs=[anywhere],
        out_specs=anywhere,
        scratch_shapes=[pltpu.VMEM(local, f32), dma((own,)), dma((own,))],
        name="store",
    )
    return store(result).reshape(fields.shape)


def solution(mesh):
    in_specs = (
        P("modes", None, "gz", None),
        P(None, "gz", None),
        P(None, None, "gz", None),
        P(),
        P(),
    )
    out_specs = P("modes", None, "gz", None)
    return jax.shard_map(body, mesh=mesh, in_specs=in_specs, out_specs=out_specs, check_vma=False)
```

```python
import functools

import jax
import jax.numpy as jnp
from jax import lax
from jax.experimental import pallas as pl
from jax.experimental.pallas import tpu as pltpu
from jax.sharding import PartitionSpec as P

CODE = 128
DEGREES = 3
UNROLL_LOW = 5
UNROLL_HIGH = 9
MESH = pl.DeviceIdType.MESH


def rank_of(index, n):
    if n % 4:
        return index
    a, q = index // 4, lax.rem(index, 4)
    p = q + (q // 2) * (1 - 2 * lax.rem(q, 2))
    return a * 4 + p + lax.rem(a, 2) * (3 - 2 * p)


def index_of(rank, n):
    if n % 4:
        return rank
    a, p = rank // 4, lax.rem(rank, 4)
    p = p + lax.rem(a, 2) * (3 - 2 * p)
    return a * 4 + p + (p // 2) * (1 - 2 * lax.rem(p, 2))


def partner(me, i, n, sign):
    if n & (n - 1):
        return lax.rem(me + sign * (i + 1) + n, n)
    odd = lax.rem(i, 2)
    step = (1 - odd) * (n // 2 + i // 2) + odd * ((i + 1) // 2)
    bit = 1
    other = me
    while bit < n:
        other = other + bit * lax.rem(step // bit, 2) * (1 - 2 * lax.rem(me // bit, 2))
        bit *= 2
    return other


def side_tiles(rows, depth):
    y_high = 0 if rows > 1 else 1
    z_low = y_high + 1
    z_high = z_low if depth > 1 else z_low + 1
    return (0, y_high, z_low, z_high), z_high + 1


def operator_kernel(n, g, rows, depth, modes, terms, slots, fields, mean, random, couple_in,
                    out, held, y_halo, z_halo, low_out, outs, couple, codes, coef, coef_halo, ctab,
                    up_v, down_v, high_v, up, down, high, own_sem, send_sem, recv_sem, back_send,
                    back_recv, ysend, yrecv, zsend, zrecv, csend, crecv, csem, tsem):
    me, layer = lax.axis_index("modes"), lax.axis_index("gz")
    own, lines = fields.shape[0], rows * depth
    lanes = fields.shape[3]
    rank = rank_of(me, n)
    before = index_of(lax.max(rank - 1, 0), n)
    after = index_of(lax.min(rank + 1, n - 1), n)
    tiles, tile_count = side_tiles(rows, depth)
    has = (rank > 0, rank < n - 1, layer > 0, layer < g - 1)
    to = ((before, layer), (after, layer), (me, layer - 1), (me, layer + 1))
    last = (rows - 1) * depth

    def pieces(side, first, count):
        return (
            [(0, depth, tiles[1], last)],
            [(last, depth, tiles[0], 0)],
            [((first + r) * depth, 1, tiles[3], (first + r) * depth + depth - 1) for r in range(count)],
            [((first + r) * depth + depth - 1, 1, tiles[2], (first + r) * depth) for r in range(count)],
        )[side]

    source_side = (1, 0, 3, 2)
    y_tiles, z_tiles = sorted(set(tiles[:2])), sorted(set(tiles[2:]))

    barrier = pltpu.get_barrier_semaphore()

    @pl.loop(1, n)
    def _(step):
        pl.semaphore_signal(barrier, inc=1, device_id=(lax.rem(me + step, n), layer),
                            device_id_type=MESH)

    @pl.loop(1, g)
    def _(step):
        pl.semaphore_signal(barrier, inc=1, device_id=(me, lax.rem(layer + step, g)),
                            device_id_type=MESH)

    pl.semaphore_wait(barrier, n + g - 2)

    def block_copy(i):
        target = partner(me, i, n, 1)
        return pltpu.make_async_remote_copy(
            src_ref=fields.at[:, rank_of(target, n)], dst_ref=held.at[pl.ds(me * own, own), 0],
            send_sem=send_sem.at[i], recv_sem=recv_sem.at[i],
            device_id=(target, layer), device_id_type=MESH)

    def block_arrived(i):
        source = partner(me, i, n, -1)
        pltpu.make_async_remote_copy(
            src_ref=fields.at[:, rank], dst_ref=held.at[pl.ds(source * own, own), 0],
            send_sem=send_sem.at[i], recv_sem=recv_sem.at[i],
            device_id=(source, layer), device_id_type=MESH).wait_recv()

    def own_copy():
        return pltpu.make_async_copy(
            fields.at[:, rank], held.at[pl.ds(me * own, own), 0], own_sem.at[0])

    def y_copy(side):
        (line, count, tile, land), = pieces(side, 0, rows)
        return pltpu.make_async_remote_copy(
            src_ref=held.at[:, 0, pl.ds(line, count)], dst_ref=y_halo.at[:, tile, pl.ds(land, count)],
            send_sem=ysend.at[side], recv_sem=yrecv.at[side], device_id=to[side], device_id_type=MESH)

    def z_copies(side, source):
        block = pl.ds(source * own, own)
        return [pltpu.make_async_remote_copy(
            src_ref=held.at[block, 0, pl.ds(line, count)],
            dst_ref=z_halo.at[block, tile - z_tiles[0], pl.ds(land, count)],
            send_sem=zsend.at[side - 2, source, j], recv_sem=zrecv.at[side - 2, source, j],
            device_id=to[side], device_id_type=MESH)
            for j, (line, count, tile, land) in enumerate(pieces(side, 0, rows))]

    def coef_copies(side):
        copies = []
        for j, (line, count, tile, land) in enumerate(pieces(side, 0, rows)):
            for part, (src, dst) in enumerate((
                    (mean.at[:, rank, pl.ds(line, count)], coef_halo.at[tile, pl.ds(0, 1), pl.ds(land, count)]),
                    (random.at[:, rank, pl.ds(line, count)], coef_halo.at[tile, pl.ds(1, terms), pl.ds(land, count)]))):
                copies.append(pltpu.make_async_remote_copy(
                    src_ref=src, dst_ref=dst, send_sem=csend.at[side - 2, j, part],
                    recv_sem=crecv.at[side - 2, j, part], device_id=to[side], device_id_type=MESH))
        return copies

    @pl.loop(0, n - 1)
    def _(i):
        block_copy(i).start()

    own_copy().start()
    local = [
        pltpu.make_async_copy(couple_in, couple, csem.at[0]),
        pltpu.make_async_copy(mean.at[:, rank], coef.at[pl.ds(0, 1)], csem.at[1]),
        pltpu.make_async_copy(random.at[:, rank], coef.at[pl.ds(1, terms)], csem.at[2]),
    ]
    for copy in local:
        copy.start()

    def row_copies(side):
        line, count, tile, land = pieces(source_side[side], 0, rows)[0]
        there = lax.max(rank - 1, 0) if side == 0 else lax.min(rank + 1, n - 1)
        return [
            pltpu.make_async_copy(mean.at[:, there, pl.ds(line, count)],
                                  coef_halo.at[tile, pl.ds(0, 1), pl.ds(land, count)], csem.at[3 + side]),
            pltpu.make_async_copy(random.at[:, there, pl.ds(line, count)],
                                  coef_halo.at[tile, pl.ds(1, terms), pl.ds(land, count)], csem.at[5 + side])]

    for side in (0, 1):
        @pl.when(has[side])
        def _():
            for copy in row_copies(side):
                copy.start()
    for side in (2, 3):
        @pl.when(has[side])
        def _():
            for copy in coef_copies(side):
                copy.start()

    def send_z(source):
        for side in (2, 3):
            @pl.when(has[side])
            def _():
                for copy in z_copies(side, source):
                    copy.start()

    local[0].wait()
    sub = lax.broadcasted_iota(jnp.int32, (8, lanes), 0)
    lane8 = lax.broadcasted_iota(jnp.int32, (8, lanes), 1)
    pairs = couple.shape[1]
    highest = (n * own - 1) * CODE + terms * DEGREES
    linear = 1 + terms
    square = linear + terms * (terms + 1) // 2

    def slot_block(b, total):
        mode = b * 8 + sub[:, :1]
        slot = jnp.zeros((8, 1), jnp.int32)
        for r in range(8):
            slot = jnp.where(sub[:, :1] == r, slots[jnp.minimum(b * 8 + r, modes - 1)], slot)
        return tuple(t + jnp.where(couple[j:j + 1, :] == mode, slot, 0) for j, t in enumerate(total))

    zeros = jnp.zeros((8, pairs), jnp.int32)
    found = lax.fori_loop(0, -(-modes // 8), slot_block, (zeros, zeros))
    target_slot, source_slot = (jnp.sum(f, axis=0, keepdims=True) for f in found)
    term = couple[2:3, :]
    index = jnp.where(term > 0, (term - 1) * DEGREES + couple[3:4, :] + 1, 0)
    codes[0:1, :] = source_slot * CODE + index
    codes[1:2, :] = target_slot

    def block_of(b):
        return b * 8 + lax.broadcasted_iota(jnp.int32, (8, 1), 0)

    def write(ref, b, values):
        table = jnp.zeros((8, lanes), jnp.int32)
        for k, value in enumerate(values):
            table = jnp.where(lane8 == k, value, table)
        ref[pl.ds(pl.multiple_of(b * 8, 8), 8), :] = jnp.clip(table, 0, highest)

    def lower(mask):
        code, big = codes[0:1, :], 2 ** 23
        mask = mask & (couple[1:2, :] < couple[0:1, :])
        low = jnp.min(jnp.where(mask, code, big), axis=1, keepdims=True)
        high = jnp.max(jnp.where(mask, code, -1), axis=1, keepdims=True)
        total = jnp.sum(jnp.where(mask, code, 0), axis=1, keepdims=True)
        middle = jnp.maximum(total - low - high, 0)
        return [jnp.where(low < big, low, 0), jnp.where(high > low, high, 0), middle]

    @pl.loop(0, up_v.shape[0] // 8)
    def _(b):
        here = couple[0:1, :] == block_of(b)
        code = jnp.where(here & (couple[1:2, :] > couple[0:1, :]), codes[0:1, :], 0)
        write(up_v, b, [jnp.sum(jnp.where(couple[2:3, :] == k + 1, code, 0), axis=1, keepdims=True)
                        for k in range(terms)])
        write(down_v, b, lower(here))

    @pl.loop(0, high_v.shape[0] // 8)
    def _(b):
        here = codes[1:2, :] == block_of(b)
        mode = jnp.where(here & (couple[2:3, :] == 0), couple[0:1, :] - modes, 0)
        mode = jnp.sum(mode, axis=1, keepdims=True) + modes
        is_high = (mode >= square) & (mode < modes)
        write(high_v, b, lower(here) + [jnp.clip(mode, 0, square), jnp.where(is_high, 1, 0)])

    moves = [pltpu.make_async_copy(a, b, tsem.at[i])
             for i, (a, b) in enumerate(((up_v, up), (down_v, down), (high_v, high)))]
    for move in moves:
        move.start()

    line = lax.broadcasted_iota(jnp.int32, (1, lines, lanes), 1)
    lane = lax.broadcasted_iota(jnp.int32, (1, lines, lanes), 2)
    row, deep = line // depth, lax.rem(line, depth)
    side_masks = (
        (row == 0) & has[0], (row == rows - 1) & has[1],
        (deep == 0) & has[2], (deep == depth - 1) & has[3],
    )

    def differences(value):
        total = 6.0 * value
        if rows > 1:
            total -= jnp.where(row == 0, 0.0, pltpu.roll(value, depth, 1))
            total -= jnp.where(row == rows - 1, 0.0, pltpu.roll(value, lines - depth, 1))
        if depth > 1:
            up_one, down_one = pltpu.roll(value, 1, 1), pltpu.roll(value, lines - 1, 1)
            if depth == 2:
                total -= jnp.where(deep == 0, down_one, up_one)
            else:
                total -= jnp.where(deep == 0, 0.0, up_one) + jnp.where(deep == depth - 1, 0.0, down_one)
        total -= jnp.where(lane == 0, 0.0, pltpu.roll(value, 1, 2))
        total -= jnp.where(lane == lanes - 1, 0.0, pltpu.roll(value, lanes - 1, 2))
        return total

    masks = []
    for tile in range(tile_count):
        sides = [side_masks[side] for side in range(4) if tiles[side] == tile]
        masks.append(functools.reduce(jnp.logical_or, sides))

    for copy in local[1:]:
        copy.wait()
    for side in (0, 1):
        @pl.when(has[side])
        def _():
            for copy in row_copies(side):
                copy.wait()
    for side in (2, 3):
        @pl.when(has[side])
        def _():
            for copy in coef_copies(side):
                copy.wait_send()

        @pl.when(has[source_side[side]])
        def _():
            for copy in coef_copies(side):
                copy.wait_recv()

    here = coef[...]
    beyond = [jnp.where(masks[tile], coef_halo[tile], 0.0) for tile in range(tile_count)]
    spread = differences(here) - sum(beyond)
    faces = [jnp.where(masks[tile], here + beyond[tile], 0.0) for tile in range(tile_count)]
    diagonal = terms * DEGREES + 1

    def put(place, k, weight):
        for j, value in enumerate((here, *faces, spread)):
            ctab[place, j] = weight * value[k]

    zero = jnp.zeros((lines, lanes), jnp.float32)
    for j in range(tile_count + 2):
        ctab[0, j] = zero
    for k in range(terms):
        for d in range(DEGREES):
            degree = jnp.full((1, 1), d, jnp.float32)
            weight = (degree + 1.0) * lax.rsqrt((2.0 * degree + 1.0) * (2.0 * degree + 3.0))
            put(k * DEGREES + d + 1, k + 1, 0.5 * weight)
    put(diagonal, 0, 0.5)

    def arrived(source):
        send_z(source)
        block = pl.ds(source * own, own)
        held[block, 1] = differences(held[block, 0])

    own_copy().wait()
    arrived(me)

    @pl.loop(0, n - 1)
    def _(i):
        block_arrived(i)
        arrived(partner(me, i, n, -1))

    for side in (0, 1):
        @pl.when(has[side])
        def _():
            y_copy(side).start()

    def main_terms(slot, place):
        value, c = held[slot, 0], ctab[place, 0]
        return [c * value, c * held[slot, 1] - ctab[place, tile_count + 1] * value]

    def outer_terms(some):
        halo = y_halo if some is y_tiles else z_halo
        return lambda slot, place: [ctab[place, 1 + t] * halo[slot, t - some[0]] for t in some]

    def both_terms(slot, place):
        return main_terms(slot, place) + outer_terms(z_tiles)(slot, place)

    def summed(term_of, slot, codes_of):
        total = term_of(slot, diagonal)
        for code in codes_of:
            new = term_of(lax.shift_right_logical(code, 7), code & (CODE - 1))
            total = [a + b for a, b in zip(total, new)]
        return total

    def inner(totals):
        product, other = (jnp.stack(part) for part in zip(*(total[:2] for total in totals)))
        result = differences(product) + other
        return [result[u] for u in range(len(totals))]

    def outer(total, some):
        return sum(jnp.where(masks[t][0], part, 0.0) for t, part in zip(some, total))

    def low_group(stage, first, count, ups, downs):
        term_of = (main_terms, outer_terms(z_tiles), outer_terms(y_tiles))[stage]
        totals = [summed(term_of, slots[first + u],
                         [up[first + u, k] for k in range(ups)] + [down[first + u, k] for k in range(downs)])
                  for u in range(count)]
        if stage == 0:
            result = inner(totals)
        else:
            result = [outer(total, z_tiles if stage == 1 else y_tiles) for total in totals]
        if stage == 1:
            result = [low_out[0, first + u] - result[u] for u in range(count)]
        for u in range(count):
            low_out[stage // 2, first + u] = result[u]

    def level(stage, first, stop, downs, unroll):
        whole = (stop - first) // unroll

        @pl.loop(0, whole)
        def _(b):
            low_group(stage, first + b * unroll, unroll, terms, downs)

        if first + whole * unroll < stop:
            low_group(stage, first + whole * unroll, stop - first - whole * unroll, terms, downs)

    def all_low(stage):
        level(stage, 0, 1, 0, 1)
        level(stage, 1, linear, 1, UNROLL_LOW)
        level(stage, linear, square, 2, UNROLL_LOW)

    def slot_group(stage, first, count):
        term_of = (both_terms, outer_terms(y_tiles))[stage]
        totals = [summed(term_of, first + u, [high[first + u, k] for k in range(DEGREES)])
                  for u in range(count)]
        if stage == 0:
            result = [a - outer(total[2:], z_tiles) for a, total in zip(inner(totals), totals)]
        else:
            result = [outer(total, y_tiles) for total in totals]
        result = [jnp.where(high[first + u, 4] > 0, result[u], low_out[stage, high[first + u, 3]])
                  for u in range(count)]
        if stage == 1:
            result = [outs[0, first + u] - result[u] for u in range(count)]
        for u in range(count):
            outs[stage, first + u] = result[u]

    def owner(stage, target):
        unroll = max(u for u in range(1, UNROLL_HIGH + 1) if own % u == 0)

        @pl.loop(0, own // unroll)
        def _(b):
            slot_group(stage, target * own + b * unroll, unroll)

    if rows > 2:
        spans = ((pl.ds(depth, lines - 2 * depth),), (pl.ds(0, depth), pl.ds(last, depth)))
    else:
        spans = ((), (pl.ds(0, lines),))

    def back_copies(stage, i, leaving):
        target, source = partner(me, i, n, 1), partner(me, i, n, -1)
        held_by, block = (target, rank) if leaving else (me, rank_of(source, n))
        first = stage * len(spans[0])
        return [pltpu.make_async_remote_copy(
            src_ref=outs.at[stage, pl.ds(held_by * own, own), span], dst_ref=out.at[:, block, span],
            send_sem=back_send.at[first + j, i], recv_sem=back_recv.at[first + j, i],
            device_id=(target, layer), device_id_type=MESH) for j, span in enumerate(spans[stage])]

    def own_back(stage):
        first = stage * len(spans[0])
        return [pltpu.make_async_copy(
            outs.at[stage, pl.ds(me * own, own), span], out.at[:, rank, span], own_sem.at[1 + first + j])
            for j, span in enumerate(spans[stage])]

    for move in moves:
        move.wait()
    for stage in range(2):
        low_out[stage, square] = zero
    all_low(0)
    for side in (2, 3):
        @pl.when(has[source_side[side]])
        def _():
            @pl.loop(0, n)
            def _(source):
                for copy in z_copies(side, source):
                    copy.wait_recv()
    all_low(1)

    for stage in range(2):
        if stage == 1:
            for side in (0, 1):
                @pl.when(has[source_side[side]])
                def _():
                    y_copy(side).wait_recv()
            all_low(2)

        @pl.loop(0, n - 1)
        def _(i):
            owner(stage, partner(me, i, n, 1))
            for copy in back_copies(stage, i, True):
                copy.start()

        owner(stage, me)
        for copy in own_back(stage):
            copy.start()

    @pl.loop(0, n - 1)
    def _(i):
        block_copy(i).wait_send()

    for side in (2, 3):
        @pl.when(has[side])
        def _():
            @pl.loop(0, n)
            def _(source):
                for copy in z_copies(side, source):
                    copy.wait_send()
    for side in (0, 1):
        @pl.when(has[side])
        def _():
            y_copy(side).wait_send()
    for stage in range(2):
        for copy in own_back(stage):
            copy.wait()

        @pl.loop(0, n - 1)
        def _(i):
            for copy in back_copies(stage, i, False):
                copy.wait_recv()
            for copy in back_copies(stage, i, True):
                copy.wait_send()


def store_kernel(source, out, held, into, back):
    count = source.shape[0]
    for i in range(count):
        pltpu.make_async_copy(source.at[i], held.at[i], into.at[i]).start()
    for i in range(count):
        pltpu.make_async_copy(source.at[i], held.at[i], into.at[i]).wait()
        pltpu.make_async_copy(held.at[i], out.at[i], back.at[i]).start()
    for i in range(count):
        pltpu.make_async_copy(held.at[i], out.at[i], back.at[i]).wait()


def body(fields, mean_coeff, random_coeff, coupling, mode_slots):
    n, g = lax.axis_size("modes"), lax.axis_size("gz")
    own, row_total, depth, across = fields.shape
    rows = row_total // n
    lines = rows * depth
    terms = random_coeff.shape[0]
    modes, pairs = mode_slots.shape[0], coupling.shape[0]
    f32, i32 = jnp.float32, jnp.int32
    smem = pl.BlockSpec(memory_space=pltpu.SMEM)
    anywhere = pl.BlockSpec(memory_space=pl.ANY)
    dma = pltpu.SemaphoreType.DMA
    tiles, tile_count = side_tiles(rows, depth)
    y_count = tiles[2]
    places = terms * DEGREES + 2
    low_modes = 1 + terms + terms * (terms + 1) // 2
    low_rows = -(-low_modes // 8) * 8
    slot_rows = -(-n * own // 8) * 8

    def tile(*lead):
        return pltpu.VMEM((*lead, lines, across), f32)

    local = (own, n, lines, across)
    operator = pl.pallas_call(
        functools.partial(operator_kernel, n, g, rows, depth, modes, terms),
        out_shape=jax.ShapeDtypeStruct(local, f32),
        in_specs=[smem] + [anywhere] * 4,
        out_specs=anywhere,
        scratch_shapes=[
            tile(n * own, 2), tile(n * own, y_count), tile(n * own, tile_count - y_count),
            tile(2, low_modes + 1), tile(2, n * own),
            pltpu.VMEM((4, pairs), i32), pltpu.VMEM((2, pairs), i32),
            tile(terms + 1), tile(tile_count, terms + 1), tile(places, tile_count + 2),
            *(pltpu.VMEM((size, across), i32) for size in (low_rows, low_rows, slot_rows)),
            *(pltpu.SMEM((size, across), i32) for size in (low_rows, low_rows, slot_rows)),
            dma((4,)), dma((n - 1,)), dma((n - 1,)), dma((3, n - 1)), dma((3, n - 1)),
            dma((2,)), dma((2,)), dma((2, n, rows)), dma((2, n, rows)), dma((2, rows, 2)), dma((2, rows, 2)),
            dma((7,)), dma((3,)),
        ],
        compiler_params=pltpu.CompilerParams(collective_id=0, has_side_effects=True),
        name="operator",
    )
    result = operator(
        mode_slots, fields.reshape(local), mean_coeff.reshape(1, n, lines, across),
        random_coeff.reshape(terms, n, lines, across), coupling.T)

    store = pl.pallas_call(
        store_kernel,
        out_shape=jax.ShapeDtypeStruct(local, f32),
        in_specs=[anywhere],
        out_specs=anywhere,
        scratch_shapes=[pltpu.VMEM(local, f32), dma((own,)), dma((own,))],
        name="store",
    )
    return store(result).reshape(fields.shape)


def solution(mesh):
    in_specs = (
        P("modes", None, "gz", None),
        P(None, "gz", None),
        P(None, None, "gz", None),
        P(),
        P(),
    )
    out_specs = P("modes", None, "gz", None)
    return jax.shard_map(body, mesh=mesh, in_specs=in_specs, out_specs=out_specs, check_vma=False)
```

```python
import functools

import jax
import jax.numpy as jnp
from jax import lax
from jax.experimental import pallas as pl
from jax.experimental.pallas import tpu as pltpu
from jax.sharding import PartitionSpec as P

CODE = 128
DEGREES = 3
UNROLL_LOW = 5
UNROLL_HIGH = 9
MESH = pl.DeviceIdType.MESH


def rank_of(index, n):
    if n % 4:
        return index
    a, q = index // 4, lax.rem(index, 4)
    p = q + (q // 2) * (1 - 2 * lax.rem(q, 2))
    return a * 4 + p + lax.rem(a, 2) * (3 - 2 * p)


def index_of(rank, n):
    if n % 4:
        return rank
    a, p = rank // 4, lax.rem(rank, 4)
    p = p + lax.rem(a, 2) * (3 - 2 * p)
    return a * 4 + p + (p // 2) * (1 - 2 * lax.rem(p, 2))


def partner(me, i, n, sign):
    if n & (n - 1):
        return lax.rem(me + sign * (i + 1) + n, n)
    odd = lax.rem(i, 2)
    step = (1 - odd) * (n - 1 - i // 2) + odd * (n // 2 - (i + 1) // 2)
    bit = 1
    other = me
    while bit < n:
        other = other + bit * lax.rem(step // bit, 2) * (1 - 2 * lax.rem(me // bit, 2))
        bit *= 2
    return other


def side_tiles(rows, depth):
    y_high = 0 if rows > 1 else 1
    z_low = y_high + 1
    z_high = z_low if depth > 1 else z_low + 1
    return (0, y_high, z_low, z_high), z_high + 1


def operator_kernel(n, g, rows, depth, modes, terms, slots, fields, mean, random, couple_in,
                    out, held, y_halo, z_halo, low_out, outs, couple, codes, coef, coef_halo, ctab,
                    up_v, down_v, high_v, up, down, high, own_sem, send_sem, recv_sem, back_send,
                    back_recv, ysend, yrecv, zsend, zrecv, csend, crecv, csem, tsem):
    me, layer = lax.axis_index("modes"), lax.axis_index("gz")
    own, lines = fields.shape[0], rows * depth
    lanes = fields.shape[3]
    rank = rank_of(me, n)
    before = index_of(lax.max(rank - 1, 0), n)
    after = index_of(lax.min(rank + 1, n - 1), n)
    tiles, tile_count = side_tiles(rows, depth)
    has = (rank > 0, rank < n - 1, layer > 0, layer < g - 1)
    to = ((before, layer), (after, layer), (me, layer - 1), (me, layer + 1))
    last = (rows - 1) * depth

    def pieces(side, first, count):
        return (
            [(0, depth, tiles[1], last)],
            [(last, depth, tiles[0], 0)],
            [((first + r) * depth, 1, tiles[3], (first + r) * depth + depth - 1) for r in range(count)],
            [((first + r) * depth + depth - 1, 1, tiles[2], (first + r) * depth) for r in range(count)],
        )[side]

    source_side = (1, 0, 3, 2)
    y_tiles, z_tiles = sorted(set(tiles[:2])), sorted(set(tiles[2:]))

    barrier = pltpu.get_barrier_semaphore()

    @pl.loop(1, n)
    def _(step):
        pl.semaphore_signal(barrier, inc=1, device_id=(lax.rem(me + step, n), layer),
                            device_id_type=MESH)

    @pl.loop(1, g)
    def _(step):
        pl.semaphore_signal(barrier, inc=1, device_id=(me, lax.rem(layer + step, g)),
                            device_id_type=MESH)

    pl.semaphore_wait(barrier, n + g - 2)

    def block_copy(i):
        target = partner(me, i, n, 1)
        return pltpu.make_async_remote_copy(
            src_ref=fields.at[:, rank_of(target, n)], dst_ref=held.at[pl.ds(me * own, own), 0],
            send_sem=send_sem.at[i], recv_sem=recv_sem.at[i],
            device_id=(target, layer), device_id_type=MESH)

    def block_arrived(i):
        source = partner(me, i, n, -1)
        pltpu.make_async_remote_copy(
            src_ref=fields.at[:, rank], dst_ref=held.at[pl.ds(source * own, own), 0],
            send_sem=send_sem.at[i], recv_sem=recv_sem.at[i],
            device_id=(source, layer), device_id_type=MESH).wait_recv()

    def own_copy():
        return pltpu.make_async_copy(
            fields.at[:, rank], held.at[pl.ds(me * own, own), 0], own_sem.at[0])

    def y_copy(side):
        (line, count, tile, land), = pieces(side, 0, rows)
        return pltpu.make_async_remote_copy(
            src_ref=held.at[:, 0, pl.ds(line, count)], dst_ref=y_halo.at[:, tile, pl.ds(land, count)],
            send_sem=ysend.at[side], recv_sem=yrecv.at[side], device_id=to[side], device_id_type=MESH)

    def z_copies(side, source):
        block = pl.ds(source * own, own)
        return [pltpu.make_async_remote_copy(
            src_ref=held.at[block, 0, pl.ds(line, count)],
            dst_ref=z_halo.at[block, tile - z_tiles[0], pl.ds(land, count)],
            send_sem=zsend.at[side - 2, source, j], recv_sem=zrecv.at[side - 2, source, j],
            device_id=to[side], device_id_type=MESH)
            for j, (line, count, tile, land) in enumerate(pieces(side, 0, rows))]

    def coef_copies(side):
        copies = []
        for j, (line, count, tile, land) in enumerate(pieces(side, 0, rows)):
            for part, (src, dst) in enumerate((
                    (mean.at[:, rank, pl.ds(line, count)], coef_halo.at[tile, pl.ds(0, 1), pl.ds(land, count)]),
                    (random.at[:, rank, pl.ds(line, count)], coef_halo.at[tile, pl.ds(1, terms), pl.ds(land, count)]))):
                copies.append(pltpu.make_async_remote_copy(
                    src_ref=src, dst_ref=dst, send_sem=csend.at[side - 2, j, part],
                    recv_sem=crecv.at[side - 2, j, part], device_id=to[side], device_id_type=MESH))
        return copies

    @pl.loop(0, n - 1)
    def _(i):
        block_copy(i).start()

    own_copy().start()
    local = [
        pltpu.make_async_copy(couple_in, couple, csem.at[0]),
        pltpu.make_async_copy(mean.at[:, rank], coef.at[pl.ds(0, 1)], csem.at[1]),
        pltpu.make_async_copy(random.at[:, rank], coef.at[pl.ds(1, terms)], csem.at[2]),
    ]
    for copy in local:
        copy.start()

    def row_copies(side):
        line, count, tile, land = pieces(source_side[side], 0, rows)[0]
        there = lax.max(rank - 1, 0) if side == 0 else lax.min(rank + 1, n - 1)
        return [
            pltpu.make_async_copy(mean.at[:, there, pl.ds(line, count)],
                                  coef_halo.at[tile, pl.ds(0, 1), pl.ds(land, count)], csem.at[3 + side]),
            pltpu.make_async_copy(random.at[:, there, pl.ds(line, count)],
                                  coef_halo.at[tile, pl.ds(1, terms), pl.ds(land, count)], csem.at[5 + side])]

    for side in (0, 1):
        @pl.when(has[side])
        def _():
            for copy in row_copies(side):
                copy.start()
    for side in (2, 3):
        @pl.when(has[side])
        def _():
            for copy in coef_copies(side):
                copy.start()

    def send_z(source):
        for side in (2, 3):
            @pl.when(has[side])
            def _():
                for copy in z_copies(side, source):
                    copy.start()

    local[0].wait()
    sub = lax.broadcasted_iota(jnp.int32, (8, lanes), 0)
    lane8 = lax.broadcasted_iota(jnp.int32, (8, lanes), 1)
    pairs = couple.shape[1]
    highest = (n * own - 1) * CODE + terms * DEGREES
    linear = 1 + terms
    square = linear + terms * (terms + 1) // 2

    def slot_block(b, total):
        mode = b * 8 + sub[:, :1]
        slot = jnp.zeros((8, 1), jnp.int32)
        for r in range(8):
            slot = jnp.where(sub[:, :1] == r, slots[jnp.minimum(b * 8 + r, modes - 1)], slot)
        return tuple(t + jnp.where(couple[j:j + 1, :] == mode, slot, 0) for j, t in enumerate(total))

    zeros = jnp.zeros((8, pairs), jnp.int32)
    found = lax.fori_loop(0, -(-modes // 8), slot_block, (zeros, zeros))
    target_slot, source_slot = (jnp.sum(f, axis=0, keepdims=True) for f in found)
    term = couple[2:3, :]
    index = jnp.where(term > 0, (term - 1) * DEGREES + couple[3:4, :] + 1, 0)
    codes[0:1, :] = source_slot * CODE + index
    codes[1:2, :] = target_slot

    def block_of(b):
        return b * 8 + lax.broadcasted_iota(jnp.int32, (8, 1), 0)

    def write(ref, b, values):
        table = jnp.zeros((8, lanes), jnp.int32)
        for k, value in enumerate(values):
            table = jnp.where(lane8 == k, value, table)
        ref[pl.ds(pl.multiple_of(b * 8, 8), 8), :] = jnp.clip(table, 0, highest)

    def lower(mask):
        code, big = codes[0:1, :], 2 ** 23
        mask = mask & (couple[1:2, :] < couple[0:1, :])
        low = jnp.min(jnp.where(mask, code, big), axis=1, keepdims=True)
        high = jnp.max(jnp.where(mask, code, -1), axis=1, keepdims=True)
        total = jnp.sum(jnp.where(mask, code, 0), axis=1, keepdims=True)
        middle = jnp.maximum(total - low - high, 0)
        return [jnp.where(low < big, low, 0), jnp.where(high > low, high, 0), middle]

    @pl.loop(0, up_v.shape[0] // 8)
    def _(b):
        here = couple[0:1, :] == block_of(b)
        code = jnp.where(here & (couple[1:2, :] > couple[0:1, :]), codes[0:1, :], 0)
        write(up_v, b, [jnp.sum(jnp.where(couple[2:3, :] == k + 1, code, 0), axis=1, keepdims=True)
                        for k in range(terms)])
        write(down_v, b, lower(here))

    @pl.loop(0, high_v.shape[0] // 8)
    def _(b):
        here = codes[1:2, :] == block_of(b)
        mode = jnp.where(here & (couple[2:3, :] == 0), couple[0:1, :] - modes, 0)
        mode = jnp.sum(mode, axis=1, keepdims=True) + modes
        is_high = (mode >= square) & (mode < modes)
        write(high_v, b, lower(here) + [jnp.clip(mode, 0, square), jnp.where(is_high, 1, 0)])

    moves = [pltpu.make_async_copy(a, b, tsem.at[i])
             for i, (a, b) in enumerate(((up_v, up), (down_v, down), (high_v, high)))]
    for move in moves:
        move.start()

    line = lax.broadcasted_iota(jnp.int32, (1, lines, lanes), 1)
    lane = lax.broadcasted_iota(jnp.int32, (1, lines, lanes), 2)
    row, deep = line // depth, lax.rem(line, depth)
    side_masks = (
        (row == 0) & has[0], (row == rows - 1) & has[1],
        (deep == 0) & has[2], (deep == depth - 1) & has[3],
    )

    def differences(value):
        total = 6.0 * value
        if rows > 1:
            total -= jnp.where(row == 0, 0.0, pltpu.roll(value, depth, 1))
            total -= jnp.where(row == rows - 1, 0.0, pltpu.roll(value, lines - depth, 1))
        if depth > 1:
            up_one, down_one = pltpu.roll(value, 1, 1), pltpu.roll(value, lines - 1, 1)
            if depth == 2:
                total -= jnp.where(deep == 0, down_one, up_one)
            else:
                total -= jnp.where(deep == 0, 0.0, up_one) + jnp.where(deep == depth - 1, 0.0, down_one)
        total -= jnp.where(lane == 0, 0.0, pltpu.roll(value, 1, 2))
        total -= jnp.where(lane == lanes - 1, 0.0, pltpu.roll(value, lanes - 1, 2))
        return total

    masks = []
    for tile in range(tile_count):
        sides = [side_masks[side] for side in range(4) if tiles[side] == tile]
        masks.append(functools.reduce(jnp.logical_or, sides))

    for copy in local[1:]:
        copy.wait()
    for side in (0, 1):
        @pl.when(has[side])
        def _():
            for copy in row_copies(side):
                copy.wait()
    for side in (2, 3):
        @pl.when(has[side])
        def _():
            for copy in coef_copies(side):
                copy.wait_send()

        @pl.when(has[source_side[side]])
        def _():
            for copy in coef_copies(side):
                copy.wait_recv()

    here = coef[...]
    beyond = [jnp.where(masks[tile], coef_halo[tile], 0.0) for tile in range(tile_count)]
    spread = differences(here) - sum(beyond)
    faces = [jnp.where(masks[tile], here + beyond[tile], 0.0) for tile in range(tile_count)]
    diagonal = terms * DEGREES + 1

    def put(place, k, weight):
        for j, value in enumerate((here, *faces, spread)):
            ctab[place, j] = weight * value[k]

    zero = jnp.zeros((lines, lanes), jnp.float32)
    for j in range(tile_count + 2):
        ctab[0, j] = zero
    for k in range(terms):
        for d in range(DEGREES):
            degree = jnp.full((1, 1), d, jnp.float32)
            weight = (degree + 1.0) * lax.rsqrt((2.0 * degree + 1.0) * (2.0 * degree + 3.0))
            put(k * DEGREES + d + 1, k + 1, 0.5 * weight)
    put(diagonal, 0, 0.5)

    def arrived(source):
        send_z(source)
        block = pl.ds(source * own, own)
        held[block, 1] = differences(held[block, 0])

    own_copy().wait()
    arrived(me)

    @pl.loop(0, n - 1)
    def _(i):
        block_arrived(i)
        arrived(partner(me, i, n, -1))

    for side in (0, 1):
        @pl.when(has[side])
        def _():
            y_copy(side).start()

    def main_terms(slot, place):
        value, c = held[slot, 0], ctab[place, 0]
        return [c * value, c * held[slot, 1] - ctab[place, tile_count + 1] * value]

    def outer_terms(some):
        halo = y_halo if some is y_tiles else z_halo
        return lambda slot, place: [ctab[place, 1 + t] * halo[slot, t - some[0]] for t in some]

    def both_terms(slot, place):
        return main_terms(slot, place) + outer_terms(z_tiles)(slot, place)

    def summed(term_of, slot, codes_of):
        total = term_of(slot, diagonal)
        for code in codes_of:
            new = term_of(lax.shift_right_logical(code, 7), code & (CODE - 1))
            total = [a + b for a, b in zip(total, new)]
        return total

    def inner(totals):
        product, other = (jnp.stack(part) for part in zip(*(total[:2] for total in totals)))
        result = differences(product) + other
        return [result[u] for u in range(len(totals))]

    def outer(total, some):
        return sum(jnp.where(masks[t][0], part, 0.0) for t, part in zip(some, total))

    def low_group(stage, first, count, ups, downs):
        term_of = (main_terms, outer_terms(z_tiles), outer_terms(y_tiles))[stage]
        totals = [summed(term_of, slots[first + u],
                         [up[first + u, k] for k in range(ups)] + [down[first + u, k] for k in range(downs)])
                  for u in range(count)]
        if stage == 0:
            result = inner(totals)
        else:
            result = [outer(total, z_tiles if stage == 1 else y_tiles) for total in totals]
        if stage == 1:
            result = [low_out[0, first + u] - result[u] for u in range(count)]
        for u in range(count):
            low_out[stage // 2, first + u] = result[u]

    def level(stage, first, stop, downs, unroll):
        whole = (stop - first) // unroll

        @pl.loop(0, whole)
        def _(b):
            low_group(stage, first + b * unroll, unroll, terms, downs)

        if first + whole * unroll < stop:
            low_group(stage, first + whole * unroll, stop - first - whole * unroll, terms, downs)

    def all_low(stage):
        level(stage, 0, 1, 0, 1)
        level(stage, 1, linear, 1, UNROLL_LOW)
        level(stage, linear, square, 2, UNROLL_LOW)

    def slot_group(stage, first, count):
        term_of = (both_terms, outer_terms(y_tiles))[stage]
        totals = [summed(term_of, first + u, [high[first + u, k] for k in range(DEGREES)])
                  for u in range(count)]
        if stage == 0:
            result = [a - outer(total[2:], z_tiles) for a, total in zip(inner(totals), totals)]
        else:
            result = [outer(total, y_tiles) for total in totals]
        result = [jnp.where(high[first + u, 4] > 0, result[u], low_out[stage, high[first + u, 3]])
                  for u in range(count)]
        if stage == 1:
            result = [outs[0, first + u] - result[u] for u in range(count)]
        for u in range(count):
            outs[stage, first + u] = result[u]

    def owner(stage, target):
        unroll = max(u for u in range(1, UNROLL_HIGH + 1) if own % u == 0)

        @pl.loop(0, own // unroll)
        def _(b):
            slot_group(stage, target * own + b * unroll, unroll)

    if rows > 2:
        spans = ((pl.ds(depth, lines - 2 * depth),), (pl.ds(0, depth), pl.ds(last, depth)))
    else:
        spans = ((), (pl.ds(0, lines),))

    def back_copies(stage, i, leaving):
        target, source = partner(me, i, n, 1), partner(me, i, n, -1)
        held_by, block = (target, rank) if leaving else (me, rank_of(source, n))
        first = stage * len(spans[0])
        return [pltpu.make_async_remote_copy(
            src_ref=outs.at[stage, pl.ds(held_by * own, own), span], dst_ref=out.at[:, block, span],
            send_sem=back_send.at[first + j, i], recv_sem=back_recv.at[first + j, i],
            device_id=(target, layer), device_id_type=MESH) for j, span in enumerate(spans[stage])]

    def own_back(stage):
        first = stage * len(spans[0])
        return [pltpu.make_async_copy(
            outs.at[stage, pl.ds(me * own, own), span], out.at[:, rank, span], own_sem.at[1 + first + j])
            for j, span in enumerate(spans[stage])]

    for move in moves:
        move.wait()
    for stage in range(2):
        low_out[stage, square] = zero
    all_low(0)
    for side in (2, 3):
        @pl.when(has[source_side[side]])
        def _():
            @pl.loop(0, n)
            def _(source):
                for copy in z_copies(side, source):
                    copy.wait_recv()
    all_low(1)

    for stage in range(2):
        if stage == 1:
            for side in (0, 1):
                @pl.when(has[source_side[side]])
                def _():
                    y_copy(side).wait_recv()
            all_low(2)

        @pl.loop(0, n - 1)
        def _(i):
            owner(stage, partner(me, i, n, 1))
            for copy in back_copies(stage, i, True):
                copy.start()

        owner(stage, me)
        for copy in own_back(stage):
            copy.start()

    @pl.loop(0, n - 1)
    def _(i):
        block_copy(i).wait_send()

    for side in (2, 3):
        @pl.when(has[side])
        def _():
            @pl.loop(0, n)
            def _(source):
                for copy in z_copies(side, source):
                    copy.wait_send()
    for side in (0, 1):
        @pl.when(has[side])
        def _():
            y_copy(side).wait_send()
    for stage in range(2):
        for copy in own_back(stage):
            copy.wait()

        @pl.loop(0, n - 1)
        def _(i):
            for copy in back_copies(stage, i, False):
                copy.wait_recv()
            for copy in back_copies(stage, i, True):
                copy.wait_send()


def store_kernel(source, out, held, into, back):
    count = source.shape[0]
    for i in range(count):
        pltpu.make_async_copy(source.at[i], held.at[i], into.at[i]).start()
    for i in range(count):
        pltpu.make_async_copy(source.at[i], held.at[i], into.at[i]).wait()
        pltpu.make_async_copy(held.at[i], out.at[i], back.at[i]).start()
    for i in range(count):
        pltpu.make_async_copy(held.at[i], out.at[i], back.at[i]).wait()


def body(fields, mean_coeff, random_coeff, coupling, mode_slots):
    n, g = lax.axis_size("modes"), lax.axis_size("gz")
    own, row_total, depth, across = fields.shape
    rows = row_total // n
    lines = rows * depth
    terms = random_coeff.shape[0]
    modes, pairs = mode_slots.shape[0], coupling.shape[0]
    f32, i32 = jnp.float32, jnp.int32
    smem = pl.BlockSpec(memory_space=pltpu.SMEM)
    anywhere = pl.BlockSpec(memory_space=pl.ANY)
    dma = pltpu.SemaphoreType.DMA
    tiles, tile_count = side_tiles(rows, depth)
    y_count = tiles[2]
    places = terms * DEGREES + 2
    low_modes = 1 + terms + terms * (terms + 1) // 2
    low_rows = -(-low_modes // 8) * 8
    slot_rows = -(-n * own // 8) * 8

    def tile(*lead):
        return pltpu.VMEM((*lead, lines, across), f32)

    local = (own, n, lines, across)
    operator = pl.pallas_call(
        functools.partial(operator_kernel, n, g, rows, depth, modes, terms),
        out_shape=jax.ShapeDtypeStruct(local, f32),
        in_specs=[smem] + [anywhere] * 4,
        out_specs=anywhere,
        scratch_shapes=[
            tile(n * own, 2), tile(n * own, y_count), tile(n * own, tile_count - y_count),
            tile(2, low_modes + 1), tile(2, n * own),
            pltpu.VMEM((4, pairs), i32), pltpu.VMEM((2, pairs), i32),
            tile(terms + 1), tile(tile_count, terms + 1), tile(places, tile_count + 2),
            *(pltpu.VMEM((size, across), i32) for size in (low_rows, low_rows, slot_rows)),
            *(pltpu.SMEM((size, across), i32) for size in (low_rows, low_rows, slot_rows)),
            dma((4,)), dma((n - 1,)), dma((n - 1,)), dma((3, n - 1)), dma((3, n - 1)),
            dma((2,)), dma((2,)), dma((2, n, rows)), dma((2, n, rows)), dma((2, rows, 2)), dma((2, rows, 2)),
            dma((7,)), dma((3,)),
        ],
        compiler_params=pltpu.CompilerParams(collective_id=0, has_side_effects=True),
        name="operator",
    )
    result = operator(
        mode_slots, fields.reshape(local), mean_coeff.reshape(1, n, lines, across),
        random_coeff.reshape(terms, n, lines, across), coupling.T)

    store = pl.pallas_call(
        store_kernel,
        out_shape=jax.ShapeDtypeStruct(local, f32),
        in_specs=[anywhere],
        out_specs=anywhere,
        scratch_shapes=[pltpu.VMEM(local, f32), dma((own,)), dma((own,))],
        name="store",
    )
    return store(result).reshape(fields.shape)


def solution(mesh):
    in_specs = (
        P("modes", None, "gz", None),
        P(None, "gz", None),
        P(None, None, "gz", None),
        P(),
        P(),
    )
    out_specs = P("modes", None, "gz", None)
    return jax.shard_map(body, mesh=mesh, in_specs=in_specs, out_specs=out_specs, check_vma=False)
```

```python
import functools

import jax
import jax.numpy as jnp
from jax import lax
from jax.experimental import pallas as pl
from jax.experimental.pallas import tpu as pltpu
from jax.sharding import PartitionSpec as P

CODE = 128
DEGREES = 3
UNROLL_LOW = 5
UNROLL_HIGH = 9
MESH = pl.DeviceIdType.MESH


def rank_of(index, n):
    if n % 4:
        return index
    a, q = index // 4, lax.rem(index, 4)
    p = q + (q // 2) * (1 - 2 * lax.rem(q, 2))
    return a * 4 + p + lax.rem(a, 2) * (3 - 2 * p)


def index_of(rank, n):
    if n % 4:
        return rank
    a, p = rank // 4, lax.rem(rank, 4)
    p = p + lax.rem(a, 2) * (3 - 2 * p)
    return a * 4 + p + (p // 2) * (1 - 2 * lax.rem(p, 2))


def partner(me, i, n, sign):
    if n & (n - 1):
        return lax.rem(me + sign * (i + 1) + n, n)
    odd = lax.rem(i, 2)
    step = (1 - odd) * (n - 1 - i // 2) + odd * (n // 2 - (i + 1) // 2)
    bit = 1
    other = me
    while bit < n:
        other = other + bit * lax.rem(step // bit, 2) * (1 - 2 * lax.rem(me // bit, 2))
        bit *= 2
    return other


def side_tiles(rows, depth):
    y_high = 0 if rows > 1 else 1
    z_low = y_high + 1
    z_high = z_low if depth > 1 else z_low + 1
    return (0, y_high, z_low, z_high), z_high + 1


def operator_kernel(n, g, rows, depth, modes, terms, slots, fields, mean, random, couple_in,
                    out, held, y_halo, z_halo, low_out, outs, couple, codes, coef, coef_halo, ctab,
                    up_v, down_v, high_v, up, down, high, own_sem, send_sem, recv_sem, back_send,
                    back_recv, home_send, home_recv, ysend, yrecv, zsend, zrecv, csend, crecv, csem, tsem):
    me, layer = lax.axis_index("modes"), lax.axis_index("gz")
    own, lines = fields.shape[0], rows * depth
    lanes = fields.shape[3]
    rank = rank_of(me, n)
    before = index_of(lax.max(rank - 1, 0), n)
    after = index_of(lax.min(rank + 1, n - 1), n)
    tiles, tile_count = side_tiles(rows, depth)
    has = (rank > 0, rank < n - 1, layer > 0, layer < g - 1)
    to = ((before, layer), (after, layer), (me, layer - 1), (me, layer + 1))
    last = (rows - 1) * depth

    def pieces(side, first, count):
        return (
            [(0, depth, tiles[1], last)],
            [(last, depth, tiles[0], 0)],
            [((first + r) * depth, 1, tiles[3], (first + r) * depth + depth - 1) for r in range(count)],
            [((first + r) * depth + depth - 1, 1, tiles[2], (first + r) * depth) for r in range(count)],
        )[side]

    source_side = (1, 0, 3, 2)
    y_tiles, z_tiles = sorted(set(tiles[:2])), sorted(set(tiles[2:]))

    barrier = pltpu.get_barrier_semaphore()

    @pl.loop(1, n)
    def _(step):
        pl.semaphore_signal(barrier, inc=1, device_id=(lax.rem(me + step, n), layer),
                            device_id_type=MESH)

    @pl.loop(1, g)
    def _(step):
        pl.semaphore_signal(barrier, inc=1, device_id=(me, lax.rem(layer + step, g)),
                            device_id_type=MESH)

    pl.semaphore_wait(barrier, n + g - 2)

    def block_copy(i):
        target = partner(me, i, n, 1)
        return pltpu.make_async_remote_copy(
            src_ref=fields.at[:, rank_of(target, n)], dst_ref=held.at[pl.ds(me * own, own), 0],
            send_sem=send_sem.at[i], recv_sem=recv_sem.at[i],
            device_id=(target, layer), device_id_type=MESH)

    def block_arrived(i):
        source = partner(me, i, n, -1)
        pltpu.make_async_remote_copy(
            src_ref=fields.at[:, rank], dst_ref=held.at[pl.ds(source * own, own), 0],
            send_sem=send_sem.at[i], recv_sem=recv_sem.at[i],
            device_id=(source, layer), device_id_type=MESH).wait_recv()

    def own_copy():
        return pltpu.make_async_copy(
            fields.at[:, rank], held.at[pl.ds(me * own, own), 0], own_sem.at[0])

    def y_copy(side, block):
        (line, count, tile, land), = pieces(side, 0, rows)
        return pltpu.make_async_remote_copy(
            src_ref=held.at[block, 0, pl.ds(line, count)], dst_ref=y_halo.at[block, tile, pl.ds(land, count)],
            send_sem=ysend.at[side], recv_sem=yrecv.at[side], device_id=to[side], device_id_type=MESH)

    half = n // 2
    my_half = me // half
    everything, my_slots = pl.ds(0, n * own), pl.ds(my_half * half * own, half * own)
    other_slots = pl.ds((1 - my_half) * half * own, half * own)
    split = n % 8 == 0
    middle = (rank == half, rank == half - 1)
    edges = (index_of(half - 1, n), index_of(half, n))

    def y_each(side, cross_side, slots_there, act):
        if not split:
            @pl.when(has[cross_side])
            def _():
                act(y_copy(side, everything))
            return

        @pl.when(has[cross_side] & jnp.logical_not(middle[cross_side]))
        def _():
            act(y_copy(side, everything))

        @pl.when(middle[cross_side])
        def _():
            act(y_copy(side, slots_there))

    def home_row(h):
        (line, count, tile, land), = pieces(h, 0, rows)
        return (half if h == 0 else half - 1), pl.ds(line, count), tile, pl.ds(land, count)

    def home_copy(h, source):
        block, span, tile, land = home_row(h)
        return pltpu.make_async_remote_copy(
            src_ref=fields.at[:, block, span], dst_ref=y_halo.at[pl.ds(source * own, own), tile, land],
            send_sem=home_send.at[0], recv_sem=home_recv.at[source - h * half],
            device_id=(edges[h], layer), device_id_type=MESH)

    def home_own(h):
        block, span, tile, land = home_row(h)
        return pltpu.make_async_copy(
            fields.at[:, block, span], y_halo.at[pl.ds(me * own, own), tile, land], home_send.at[1])

    def z_copies(side, source):
        block = pl.ds(source * own, own)
        return [pltpu.make_async_remote_copy(
            src_ref=held.at[block, 0, pl.ds(line, count)],
            dst_ref=z_halo.at[block, tile - z_tiles[0], pl.ds(land, count)],
            send_sem=zsend.at[side - 2, source, j], recv_sem=zrecv.at[side - 2, source, j],
            device_id=to[side], device_id_type=MESH)
            for j, (line, count, tile, land) in enumerate(pieces(side, 0, rows))]

    def coef_copies(side):
        copies = []
        for j, (line, count, tile, land) in enumerate(pieces(side, 0, rows)):
            for part, (src, dst) in enumerate((
                    (mean.at[:, rank, pl.ds(line, count)], coef_halo.at[tile, pl.ds(0, 1), pl.ds(land, count)]),
                    (random.at[:, rank, pl.ds(line, count)], coef_halo.at[tile, pl.ds(1, terms), pl.ds(land, count)]))):
                copies.append(pltpu.make_async_remote_copy(
                    src_ref=src, dst_ref=dst, send_sem=csend.at[side - 2, j, part],
                    recv_sem=crecv.at[side - 2, j, part], device_id=to[side], device_id_type=MESH))
        return copies

    @pl.loop(0, n - 1)
    def _(i):
        block_copy(i).start()

    own_copy().start()
    local = [
        pltpu.make_async_copy(couple_in, couple, csem.at[0]),
        pltpu.make_async_copy(mean.at[:, rank], coef.at[pl.ds(0, 1)], csem.at[1]),
        pltpu.make_async_copy(random.at[:, rank], coef.at[pl.ds(1, terms)], csem.at[2]),
    ]
    for copy in local:
        copy.start()

    def row_copies(side):
        line, count, tile, land = pieces(source_side[side], 0, rows)[0]
        there = lax.max(rank - 1, 0) if side == 0 else lax.min(rank + 1, n - 1)
        return [
            pltpu.make_async_copy(mean.at[:, there, pl.ds(line, count)],
                                  coef_halo.at[tile, pl.ds(0, 1), pl.ds(land, count)], csem.at[3 + side]),
            pltpu.make_async_copy(random.at[:, there, pl.ds(line, count)],
                                  coef_halo.at[tile, pl.ds(1, terms), pl.ds(land, count)], csem.at[5 + side])]

    for side in (0, 1):
        @pl.when(has[side])
        def _():
            for copy in row_copies(side):
                copy.start()
    for side in (2, 3):
        @pl.when(has[side])
        def _():
            for copy in coef_copies(side):
                copy.start()

    def send_z(source):
        for side in (2, 3):
            @pl.when(has[side])
            def _():
                for copy in z_copies(side, source):
                    copy.start()

    local[0].wait()
    sub = lax.broadcasted_iota(jnp.int32, (8, lanes), 0)
    lane8 = lax.broadcasted_iota(jnp.int32, (8, lanes), 1)
    pairs = couple.shape[1]
    highest = (n * own - 1) * CODE + terms * DEGREES
    linear = 1 + terms
    square = linear + terms * (terms + 1) // 2

    def slot_block(b, total):
        mode = b * 8 + sub[:, :1]
        slot = jnp.zeros((8, 1), jnp.int32)
        for r in range(8):
            slot = jnp.where(sub[:, :1] == r, slots[jnp.minimum(b * 8 + r, modes - 1)], slot)
        return tuple(t + jnp.where(couple[j:j + 1, :] == mode, slot, 0) for j, t in enumerate(total))

    zeros = jnp.zeros((8, pairs), jnp.int32)
    found = lax.fori_loop(0, -(-modes // 8), slot_block, (zeros, zeros))
    target_slot, source_slot = (jnp.sum(f, axis=0, keepdims=True) for f in found)
    term = couple[2:3, :]
    index = jnp.where(term > 0, (term - 1) * DEGREES + couple[3:4, :] + 1, 0)
    codes[0:1, :] = source_slot * CODE + index
    codes[1:2, :] = target_slot

    def block_of(b):
        return b * 8 + lax.broadcasted_iota(jnp.int32, (8, 1), 0)

    def write(ref, b, values):
        table = jnp.zeros((8, lanes), jnp.int32)
        for k, value in enumerate(values):
            table = jnp.where(lane8 == k, value, table)
        ref[pl.ds(pl.multiple_of(b * 8, 8), 8), :] = jnp.clip(table, 0, highest)

    def lower(mask):
        code, big = codes[0:1, :], 2 ** 23
        mask = mask & (couple[1:2, :] < couple[0:1, :])
        low = jnp.min(jnp.where(mask, code, big), axis=1, keepdims=True)
        high = jnp.max(jnp.where(mask, code, -1), axis=1, keepdims=True)
        total = jnp.sum(jnp.where(mask, code, 0), axis=1, keepdims=True)
        middle = jnp.maximum(total - low - high, 0)
        return [jnp.where(low < big, low, 0), jnp.where(high > low, high, 0), middle]

    @pl.loop(0, up_v.shape[0] // 8)
    def _(b):
        here = couple[0:1, :] == block_of(b)
        code = jnp.where(here & (couple[1:2, :] > couple[0:1, :]), codes[0:1, :], 0)
        write(up_v, b, [jnp.sum(jnp.where(couple[2:3, :] == k + 1, code, 0), axis=1, keepdims=True)
                        for k in range(terms)])
        write(down_v, b, lower(here))

    @pl.loop(0, high_v.shape[0] // 8)
    def _(b):
        here = codes[1:2, :] == block_of(b)
        mode = jnp.where(here & (couple[2:3, :] == 0), couple[0:1, :] - modes, 0)
        mode = jnp.sum(mode, axis=1, keepdims=True) + modes
        is_high = (mode >= square) & (mode < modes)
        write(high_v, b, lower(here) + [jnp.clip(mode, 0, square), jnp.where(is_high, 1, 0)])

    moves = [pltpu.make_async_copy(a, b, tsem.at[i])
             for i, (a, b) in enumerate(((up_v, up), (down_v, down), (high_v, high)))]
    for move in moves:
        move.start()

    line = lax.broadcasted_iota(jnp.int32, (1, lines, lanes), 1)
    lane = lax.broadcasted_iota(jnp.int32, (1, lines, lanes), 2)
    row, deep = line // depth, lax.rem(line, depth)
    side_masks = (
        (row == 0) & has[0], (row == rows - 1) & has[1],
        (deep == 0) & has[2], (deep == depth - 1) & has[3],
    )

    def differences(value):
        total = 6.0 * value
        if rows > 1:
            total -= jnp.where(row == 0, 0.0, pltpu.roll(value, depth, 1))
            total -= jnp.where(row == rows - 1, 0.0, pltpu.roll(value, lines - depth, 1))
        if depth > 1:
            up_one, down_one = pltpu.roll(value, 1, 1), pltpu.roll(value, lines - 1, 1)
            if depth == 2:
                total -= jnp.where(deep == 0, down_one, up_one)
            else:
                total -= jnp.where(deep == 0, 0.0, up_one) + jnp.where(deep == depth - 1, 0.0, down_one)
        total -= jnp.where(lane == 0, 0.0, pltpu.roll(value, 1, 2))
        total -= jnp.where(lane == lanes - 1, 0.0, pltpu.roll(value, lanes - 1, 2))
        return total

    masks = []
    for tile in range(tile_count):
        sides = [side_masks[side] for side in range(4) if tiles[side] == tile]
        masks.append(functools.reduce(jnp.logical_or, sides))

    for copy in local[1:]:
        copy.wait()
    for side in (0, 1):
        @pl.when(has[side])
        def _():
            for copy in row_copies(side):
                copy.wait()
    for side in (2, 3):
        @pl.when(has[side])
        def _():
            for copy in coef_copies(side):
                copy.wait_send()

        @pl.when(has[source_side[side]])
        def _():
            for copy in coef_copies(side):
                copy.wait_recv()

    here = coef[...]
    beyond = [jnp.where(masks[tile], coef_halo[tile], 0.0) for tile in range(tile_count)]
    spread = differences(here) - sum(beyond)
    faces = [jnp.where(masks[tile], here + beyond[tile], 0.0) for tile in range(tile_count)]
    diagonal = terms * DEGREES + 1

    def put(place, k, weight):
        for j, value in enumerate((here, *faces, spread)):
            ctab[place, j] = weight * value[k]

    zero = jnp.zeros((lines, lanes), jnp.float32)
    for j in range(tile_count + 2):
        ctab[0, j] = zero
    for k in range(terms):
        for d in range(DEGREES):
            degree = jnp.full((1, 1), d, jnp.float32)
            weight = (degree + 1.0) * lax.rsqrt((2.0 * degree + 1.0) * (2.0 * degree + 3.0))
            put(k * DEGREES + d + 1, k + 1, 0.5 * weight)
    put(diagonal, 0, 0.5)

    def arrived(source):
        send_z(source)
        block = pl.ds(source * own, own)
        held[block, 1] = differences(held[block, 0])

    own_copy().wait()
    arrived(me)

    @pl.loop(0, n - 1)
    def _(i):
        block_arrived(i)
        arrived(partner(me, i, n, -1))

    for side in (0, 1):
        y_each(side, side, my_slots, lambda copy: copy.start())
    if split:
        for h in (0, 1):
            @pl.when((my_half == h) & (me != edges[h]))
            def _():
                home_copy(h, me).start()

            @pl.when(me == edges[h])
            def _():
                home_own(h).start()

    def main_terms(slot, place):
        value, c = held[slot, 0], ctab[place, 0]
        return [c * value, c * held[slot, 1] - ctab[place, tile_count + 1] * value]

    def outer_terms(some):
        halo = y_halo if some is y_tiles else z_halo
        return lambda slot, place: [ctab[place, 1 + t] * halo[slot, t - some[0]] for t in some]

    def both_terms(slot, place):
        return main_terms(slot, place) + outer_terms(z_tiles)(slot, place)

    def summed(term_of, slot, codes_of):
        total = term_of(slot, diagonal)
        for code in codes_of:
            new = term_of(lax.shift_right_logical(code, 7), code & (CODE - 1))
            total = [a + b for a, b in zip(total, new)]
        return total

    def inner(totals):
        product, other = (jnp.stack(part) for part in zip(*(total[:2] for total in totals)))
        result = differences(product) + other
        return [result[u] for u in range(len(totals))]

    def outer(total, some):
        return sum(jnp.where(masks[t][0], part, 0.0) for t, part in zip(some, total))

    def low_group(stage, first, count, ups, downs):
        term_of = (main_terms, outer_terms(z_tiles), outer_terms(y_tiles))[stage]
        totals = [summed(term_of, slots[first + u],
                         [up[first + u, k] for k in range(ups)] + [down[first + u, k] for k in range(downs)])
                  for u in range(count)]
        if stage == 0:
            result = inner(totals)
        else:
            result = [outer(total, z_tiles if stage == 1 else y_tiles) for total in totals]
        if stage == 1:
            result = [low_out[0, first + u] - result[u] for u in range(count)]
        for u in range(count):
            low_out[stage // 2, first + u] = result[u]

    def level(stage, first, stop, downs, unroll):
        whole = (stop - first) // unroll

        @pl.loop(0, whole)
        def _(b):
            low_group(stage, first + b * unroll, unroll, terms, downs)

        if first + whole * unroll < stop:
            low_group(stage, first + whole * unroll, stop - first - whole * unroll, terms, downs)

    def all_low(stage):
        level(stage, 0, 1, 0, 1)
        level(stage, 1, linear, 1, UNROLL_LOW)
        level(stage, linear, square, 2, UNROLL_LOW)

    def slot_group(stage, first, count):
        term_of = (both_terms, outer_terms(y_tiles))[stage]
        totals = [summed(term_of, first + u, [high[first + u, k] for k in range(DEGREES)])
                  for u in range(count)]
        if stage == 0:
            result = [a - outer(total[2:], z_tiles) for a, total in zip(inner(totals), totals)]
        else:
            result = [outer(total, y_tiles) for total in totals]
        result = [jnp.where(high[first + u, 4] > 0, result[u], low_out[stage, high[first + u, 3]])
                  for u in range(count)]
        if stage == 1:
            result = [outs[0, first + u] - result[u] for u in range(count)]
        for u in range(count):
            outs[stage, first + u] = result[u]

    def owner(stage, target):
        unroll = max(u for u in range(1, UNROLL_HIGH + 1) if own % u == 0)

        @pl.loop(0, own // unroll)
        def _(b):
            slot_group(stage, target * own + b * unroll, unroll)

    if rows > 2:
        spans = ((pl.ds(depth, lines - 2 * depth),), (pl.ds(0, depth), pl.ds(last, depth)))
    else:
        spans = ((), (pl.ds(0, lines),))

    def back_copies(stage, i, leaving):
        target, source = partner(me, i, n, 1), partner(me, i, n, -1)
        held_by, block = (target, rank) if leaving else (me, rank_of(source, n))
        first = stage * len(spans[0])
        return [pltpu.make_async_remote_copy(
            src_ref=outs.at[stage, pl.ds(held_by * own, own), span], dst_ref=out.at[:, block, span],
            send_sem=back_send.at[first + j, i], recv_sem=back_recv.at[first + j, i],
            device_id=(target, layer), device_id_type=MESH) for j, span in enumerate(spans[stage])]

    def own_back(stage):
        first = stage * len(spans[0])
        return [pltpu.make_async_copy(
            outs.at[stage, pl.ds(me * own, own), span], out.at[:, rank, span], own_sem.at[1 + first + j])
            for j, span in enumerate(spans[stage])]

    for move in moves:
        move.wait()
    for stage in range(2):
        low_out[stage, square] = zero
    all_low(0)
    for side in (2, 3):
        @pl.when(has[source_side[side]])
        def _():
            @pl.loop(0, n)
            def _(source):
                for copy in z_copies(side, source):
                    copy.wait_recv()
    all_low(1)

    for stage in range(2):
        if stage == 1:
            for side in (0, 1):
                y_each(side, source_side[side], other_slots, lambda copy: copy.wait_recv())
            if split:
                for h in (0, 1):
                    @pl.when(me == edges[h])
                    def _():
                        home_own(h).wait()

                        @pl.loop(1, half)
                        def _(j):
                            home_copy(h, h * half + lax.rem(me - h * half + j, half)).wait_recv()
            all_low(2)

        @pl.loop(0, n - 1)
        def _(i):
            owner(stage, partner(me, i, n, 1))
            for copy in back_copies(stage, i, True):
                copy.start()

        owner(stage, me)
        for copy in own_back(stage):
            copy.start()

    @pl.loop(0, n - 1)
    def _(i):
        block_copy(i).wait_send()

    for side in (2, 3):
        @pl.when(has[side])
        def _():
            @pl.loop(0, n)
            def _(source):
                for copy in z_copies(side, source):
                    copy.wait_send()
    for side in (0, 1):
        y_each(side, side, my_slots, lambda copy: copy.wait_send())
    if split:
        for h in (0, 1):
            @pl.when((my_half == h) & (me != edges[h]))
            def _():
                home_copy(h, me).wait_send()
    for stage in range(2):
        for copy in own_back(stage):
            copy.wait()

        @pl.loop(0, n - 1)
        def _(i):
            for copy in back_copies(stage, i, False):
                copy.wait_recv()
            for copy in back_copies(stage, i, True):
                copy.wait_send()


def store_kernel(source, out, held, into, back):
    count = source.shape[0]
    for i in range(count):
        pltpu.make_async_copy(source.at[i], held.at[i], into.at[i]).start()
    for i in range(count):
        pltpu.make_async_copy(source.at[i], held.at[i], into.at[i]).wait()
        pltpu.make_async_copy(held.at[i], out.at[i], back.at[i]).start()
    for i in range(count):
        pltpu.make_async_copy(held.at[i], out.at[i], back.at[i]).wait()


def body(fields, mean_coeff, random_coeff, coupling, mode_slots):
    n, g = lax.axis_size("modes"), lax.axis_size("gz")
    own, row_total, depth, across = fields.shape
    rows = row_total // n
    lines = rows * depth
    terms = random_coeff.shape[0]
    modes, pairs = mode_slots.shape[0], coupling.shape[0]
    f32, i32 = jnp.float32, jnp.int32
    smem = pl.BlockSpec(memory_space=pltpu.SMEM)
    anywhere = pl.BlockSpec(memory_space=pl.ANY)
    dma = pltpu.SemaphoreType.DMA
    tiles, tile_count = side_tiles(rows, depth)
    y_count = tiles[2]
    places = terms * DEGREES + 2
    low_modes = 1 + terms + terms * (terms + 1) // 2
    low_rows = -(-low_modes // 8) * 8
    slot_rows = -(-n * own // 8) * 8

    def tile(*lead):
        return pltpu.VMEM((*lead, lines, across), f32)

    local = (own, n, lines, across)
    operator = pl.pallas_call(
        functools.partial(operator_kernel, n, g, rows, depth, modes, terms),
        out_shape=jax.ShapeDtypeStruct(local, f32),
        in_specs=[smem] + [anywhere] * 4,
        out_specs=anywhere,
        scratch_shapes=[
            tile(n * own, 2), tile(n * own, y_count), tile(n * own, tile_count - y_count),
            tile(2, low_modes + 1), tile(2, n * own),
            pltpu.VMEM((4, pairs), i32), pltpu.VMEM((2, pairs), i32),
            tile(terms + 1), tile(tile_count, terms + 1), tile(places, tile_count + 2),
            *(pltpu.VMEM((size, across), i32) for size in (low_rows, low_rows, slot_rows)),
            *(pltpu.SMEM((size, across), i32) for size in (low_rows, low_rows, slot_rows)),
            dma((4,)), dma((n - 1,)), dma((n - 1,)), dma((3, n - 1)), dma((3, n - 1)),
            dma((2,)), dma((n,)), dma((2,)), dma((2,)), dma((2, n, rows)), dma((2, n, rows)), dma((2, rows, 2)), dma((2, rows, 2)),
            dma((7,)), dma((3,)),
        ],
        compiler_params=pltpu.CompilerParams(collective_id=0, has_side_effects=True),
        name="operator",
    )
    result = operator(
        mode_slots, fields.reshape(local), mean_coeff.reshape(1, n, lines, across),
        random_coeff.reshape(terms, n, lines, across), coupling.T)

    store = pl.pallas_call(
        store_kernel,
        out_shape=jax.ShapeDtypeStruct(local, f32),
        in_specs=[anywhere],
        out_specs=anywhere,
        scratch_shapes=[pltpu.VMEM(local, f32), dma((own,)), dma((own,))],
        name="store",
    )
    return store(result).reshape(fields.shape)


def solution(mesh):
    in_specs = (
        P("modes", None, "gz", None),
        P(None, "gz", None),
        P(None, None, "gz", None),
        P(),
        P(),
    )
    out_specs = P("modes", None, "gz", None)
    return jax.shard_map(body, mesh=mesh, in_specs=in_specs, out_specs=out_specs, check_vma=False)
```

```python
import functools

import jax
import jax.numpy as jnp
from jax import lax
from jax.experimental import pallas as pl
from jax.experimental.pallas import tpu as pltpu
from jax.sharding import PartitionSpec as P

CODE = 128
DEGREES = 3
UNROLL_LOW = 11
UNROLL_HIGH = 9
MESH = pl.DeviceIdType.MESH


def rank_of(index, n):
    if n % 4:
        return index
    a, q = index // 4, lax.rem(index, 4)
    p = q + (q // 2) * (1 - 2 * lax.rem(q, 2))
    return a * 4 + p + lax.rem(a, 2) * (3 - 2 * p)


def index_of(rank, n):
    if n % 4:
        return rank
    a, p = rank // 4, lax.rem(rank, 4)
    p = p + lax.rem(a, 2) * (3 - 2 * p)
    return a * 4 + p + (p // 2) * (1 - 2 * lax.rem(p, 2))


def partner(me, i, n, sign):
    if n & (n - 1):
        return lax.rem(me + sign * (i + 1) + n, n)
    odd = lax.rem(i, 2)
    step = (1 - odd) * (n - 1 - i // 2) + odd * (n // 2 - (i + 1) // 2)
    bit = 1
    other = me
    while bit < n:
        other = other + bit * lax.rem(step // bit, 2) * (1 - 2 * lax.rem(me // bit, 2))
        bit *= 2
    return other


def side_tiles(rows, depth):
    y_high = 0 if rows > 1 else 1
    z_low = y_high + 1
    z_high = z_low if depth > 1 else z_low + 1
    return (0, y_high, z_low, z_high), z_high + 1


def operator_kernel(n, g, rows, depth, modes, terms, slots, fields, mean, random, couple_in,
                    out, held, y_halo, z_halo, low_out, outs, couple, codes, coef, coef_halo, ctab,
                    up_v, down_v, high_v, up, down, high, own_sem, send_sem, recv_sem, back_send,
                    back_recv, home_send, home_recv, ysend, yrecv, zsend, zrecv, csend, crecv, csem, tsem):
    me, layer = lax.axis_index("modes"), lax.axis_index("gz")
    own, lines = fields.shape[0], rows * depth
    lanes = fields.shape[3]
    rank = rank_of(me, n)
    before = index_of(lax.max(rank - 1, 0), n)
    after = index_of(lax.min(rank + 1, n - 1), n)
    tiles, tile_count = side_tiles(rows, depth)
    has = (rank > 0, rank < n - 1, layer > 0, layer < g - 1)
    to = ((before, layer), (after, layer), (me, layer - 1), (me, layer + 1))
    last = (rows - 1) * depth

    def pieces(side, first, count):
        return (
            [(0, depth, tiles[1], last)],
            [(last, depth, tiles[0], 0)],
            [((first + r) * depth, 1, tiles[3], (first + r) * depth + depth - 1) for r in range(count)],
            [((first + r) * depth + depth - 1, 1, tiles[2], (first + r) * depth) for r in range(count)],
        )[side]

    source_side = (1, 0, 3, 2)
    y_tiles, z_tiles = sorted(set(tiles[:2])), sorted(set(tiles[2:]))

    barrier = pltpu.get_barrier_semaphore()

    @pl.loop(1, n)
    def _(step):
        pl.semaphore_signal(barrier, inc=1, device_id=(lax.rem(me + step, n), layer),
                            device_id_type=MESH)

    @pl.loop(1, g)
    def _(step):
        pl.semaphore_signal(barrier, inc=1, device_id=(me, lax.rem(layer + step, g)),
                            device_id_type=MESH)

    pl.semaphore_wait(barrier, n + g - 2)

    def block_copy(i):
        target = partner(me, i, n, 1)
        return pltpu.make_async_remote_copy(
            src_ref=fields.at[:, rank_of(target, n)], dst_ref=held.at[pl.ds(me * own, own), 0],
            send_sem=send_sem.at[i], recv_sem=recv_sem.at[i],
            device_id=(target, layer), device_id_type=MESH)

    def block_arrived(i):
        source = partner(me, i, n, -1)
        pltpu.make_async_remote_copy(
            src_ref=fields.at[:, rank], dst_ref=held.at[pl.ds(source * own, own), 0],
            send_sem=send_sem.at[i], recv_sem=recv_sem.at[i],
            device_id=(source, layer), device_id_type=MESH).wait_recv()

    def own_copy():
        return pltpu.make_async_copy(
            fields.at[:, rank], held.at[pl.ds(me * own, own), 0], own_sem.at[0])

    def y_copy(side, block):
        (line, count, tile, land), = pieces(side, 0, rows)
        return pltpu.make_async_remote_copy(
            src_ref=held.at[block, 0, pl.ds(line, count)], dst_ref=y_halo.at[block, tile, pl.ds(land, count)],
            send_sem=ysend.at[side], recv_sem=yrecv.at[side], device_id=to[side], device_id_type=MESH)

    half = n // 2
    my_half = me // half
    everything, my_slots = pl.ds(0, n * own), pl.ds(my_half * half * own, half * own)
    other_slots = pl.ds((1 - my_half) * half * own, half * own)
    split = n % 8 == 0
    middle = (rank == half, rank == half - 1)
    edges = (index_of(half - 1, n), index_of(half, n))

    def y_each(side, cross_side, slots_there, act):
        if not split:
            @pl.when(has[cross_side])
            def _():
                act(y_copy(side, everything))
            return

        @pl.when(has[cross_side] & jnp.logical_not(middle[cross_side]))
        def _():
            act(y_copy(side, everything))

        @pl.when(middle[cross_side])
        def _():
            act(y_copy(side, slots_there))

    def home_row(h):
        (line, count, tile, land), = pieces(h, 0, rows)
        return (half if h == 0 else half - 1), pl.ds(line, count), tile, pl.ds(land, count)

    def home_copy(h, source):
        block, span, tile, land = home_row(h)
        return pltpu.make_async_remote_copy(
            src_ref=fields.at[:, block, span], dst_ref=y_halo.at[pl.ds(source * own, own), tile, land],
            send_sem=home_send.at[0], recv_sem=home_recv.at[source - h * half],
            device_id=(edges[h], layer), device_id_type=MESH)

    def home_own(h):
        block, span, tile, land = home_row(h)
        return pltpu.make_async_copy(
            fields.at[:, block, span], y_halo.at[pl.ds(me * own, own), tile, land], home_send.at[1])

    def z_copies(side, source):
        block = pl.ds(source * own, own)
        return [pltpu.make_async_remote_copy(
            src_ref=held.at[block, 0, pl.ds(line, count)],
            dst_ref=z_halo.at[block, tile - z_tiles[0], pl.ds(land, count)],
            send_sem=zsend.at[side - 2, source, j], recv_sem=zrecv.at[side - 2, source, j],
            device_id=to[side], device_id_type=MESH)
            for j, (line, count, tile, land) in enumerate(pieces(side, 0, rows))]

    def coef_copies(side):
        copies = []
        for j, (line, count, tile, land) in enumerate(pieces(side, 0, rows)):
            for part, (src, dst) in enumerate((
                    (mean.at[:, rank, pl.ds(line, count)], coef_halo.at[tile, pl.ds(0, 1), pl.ds(land, count)]),
                    (random.at[:, rank, pl.ds(line, count)], coef_halo.at[tile, pl.ds(1, terms), pl.ds(land, count)]))):
                copies.append(pltpu.make_async_remote_copy(
                    src_ref=src, dst_ref=dst, send_sem=csend.at[side - 2, j, part],
                    recv_sem=crecv.at[side - 2, j, part], device_id=to[side], device_id_type=MESH))
        return copies

    @pl.loop(0, n - 1)
    def _(i):
        block_copy(i).start()

    own_copy().start()
    local = [
        pltpu.make_async_copy(couple_in, couple, csem.at[0]),
        pltpu.make_async_copy(mean.at[:, rank], coef.at[pl.ds(0, 1)], csem.at[1]),
        pltpu.make_async_copy(random.at[:, rank], coef.at[pl.ds(1, terms)], csem.at[2]),
    ]
    for copy in local:
        copy.start()

    def row_copies(side):
        line, count, tile, land = pieces(source_side[side], 0, rows)[0]
        there = lax.max(rank - 1, 0) if side == 0 else lax.min(rank + 1, n - 1)
        return [
            pltpu.make_async_copy(mean.at[:, there, pl.ds(line, count)],
                                  coef_halo.at[tile, pl.ds(0, 1), pl.ds(land, count)], csem.at[3 + side]),
            pltpu.make_async_copy(random.at[:, there, pl.ds(line, count)],
                                  coef_halo.at[tile, pl.ds(1, terms), pl.ds(land, count)], csem.at[5 + side])]

    for side in (0, 1):
        @pl.when(has[side])
        def _():
            for copy in row_copies(side):
                copy.start()
    for side in (2, 3):
        @pl.when(has[side])
        def _():
            for copy in coef_copies(side):
                copy.start()

    def send_z(source):
        for side in (2, 3):
            @pl.when(has[side])
            def _():
                for copy in z_copies(side, source):
                    copy.start()

    local[0].wait()
    sub = lax.broadcasted_iota(jnp.int32, (8, lanes), 0)
    lane8 = lax.broadcasted_iota(jnp.int32, (8, lanes), 1)
    pairs = couple.shape[1]
    highest = (n * own - 1) * CODE + terms * DEGREES
    linear = 1 + terms
    square = linear + terms * (terms + 1) // 2

    def slot_block(b, total):
        mode = b * 8 + sub[:, :1]
        slot = jnp.zeros((8, 1), jnp.int32)
        for r in range(8):
            slot = jnp.where(sub[:, :1] == r, slots[jnp.minimum(b * 8 + r, modes - 1)], slot)
        return tuple(t + jnp.where(couple[j:j + 1, :] == mode, slot, 0) for j, t in enumerate(total))

    zeros = jnp.zeros((8, pairs), jnp.int32)
    found = lax.fori_loop(0, -(-modes // 8), slot_block, (zeros, zeros))
    target_slot, source_slot = (jnp.sum(f, axis=0, keepdims=True) for f in found)
    term = couple[2:3, :]
    index = jnp.where(term > 0, (term - 1) * DEGREES + couple[3:4, :] + 1, 0)
    codes[0:1, :] = source_slot * CODE + index
    codes[1:2, :] = target_slot

    def block_of(b):
        return b * 8 + lax.broadcasted_iota(jnp.int32, (8, 1), 0)

    def write(ref, b, values):
        table = jnp.zeros((8, lanes), jnp.int32)
        values = [jnp.clip(value, 0, highest) for value in values]
        for k in range(0, len(values), 2):
            word = values[k]
            if k + 1 < len(values):
                word = word | lax.shift_left(values[k + 1], jnp.full_like(word, 16))
            table = jnp.where(lane8 == k // 2, word, table)
        ref[pl.ds(pl.multiple_of(b * 8, 8), 8), :] = table

    def lower(mask):
        code, big = codes[0:1, :], 2 ** 23
        mask = mask & (couple[1:2, :] < couple[0:1, :])
        low = jnp.min(jnp.where(mask, code, big), axis=1, keepdims=True)
        high = jnp.max(jnp.where(mask, code, -1), axis=1, keepdims=True)
        total = jnp.sum(jnp.where(mask, code, 0), axis=1, keepdims=True)
        middle = jnp.maximum(total - low - high, 0)
        return [jnp.where(low < big, low, 0), jnp.where(high > low, high, 0), middle]

    @pl.loop(0, up_v.shape[0] // 8)
    def _(b):
        here = couple[0:1, :] == block_of(b)
        code = jnp.where(here & (couple[1:2, :] > couple[0:1, :]), codes[0:1, :], 0)
        write(up_v, b, [jnp.sum(jnp.where(couple[2:3, :] == k + 1, code, 0), axis=1, keepdims=True)
                        for k in range(terms)])
        write(down_v, b, lower(here))

    @pl.loop(0, high_v.shape[0] // 8)
    def _(b):
        here = codes[1:2, :] == block_of(b)
        mode = jnp.where(here & (couple[2:3, :] == 0), couple[0:1, :] - modes, 0)
        mode = jnp.sum(mode, axis=1, keepdims=True) + modes
        is_high = (mode >= square) & (mode < modes)
        write(high_v, b, lower(here) + [2 * jnp.clip(mode, 0, square) + jnp.where(is_high, 1, 0)])

    moves = [pltpu.make_async_copy(a, b, tsem.at[i])
             for i, (a, b) in enumerate(((up_v, up), (down_v, down), (high_v, high)))]
    for move in moves:
        move.start()

    line = lax.broadcasted_iota(jnp.int32, (1, lines, lanes), 1)
    lane = lax.broadcasted_iota(jnp.int32, (1, lines, lanes), 2)
    row, deep = line // depth, lax.rem(line, depth)
    side_masks = (
        (row == 0) & has[0], (row == rows - 1) & has[1],
        (deep == 0) & has[2], (deep == depth - 1) & has[3],
    )

    def differences(value):
        total = 6.0 * value
        if rows > 1:
            total -= jnp.where(row == 0, 0.0, pltpu.roll(value, depth, 1))
            total -= jnp.where(row == rows - 1, 0.0, pltpu.roll(value, lines - depth, 1))
        if depth > 1:
            up_one, down_one = pltpu.roll(value, 1, 1), pltpu.roll(value, lines - 1, 1)
            if depth == 2:
                total -= jnp.where(deep == 0, down_one, up_one)
            else:
                total -= jnp.where(deep == 0, 0.0, up_one) + jnp.where(deep == depth - 1, 0.0, down_one)
        total -= jnp.where(lane == 0, 0.0, pltpu.roll(value, 1, 2))
        total -= jnp.where(lane == lanes - 1, 0.0, pltpu.roll(value, lanes - 1, 2))
        return total

    masks = []
    for tile in range(tile_count):
        sides = [side_masks[side] for side in range(4) if tiles[side] == tile]
        masks.append(functools.reduce(jnp.logical_or, sides))

    for copy in local[1:]:
        copy.wait()
    for side in (0, 1):
        @pl.when(has[side])
        def _():
            for copy in row_copies(side):
                copy.wait()
    for side in (2, 3):
        @pl.when(has[side])
        def _():
            for copy in coef_copies(side):
                copy.wait_send()

        @pl.when(has[source_side[side]])
        def _():
            for copy in coef_copies(side):
                copy.wait_recv()

    here = coef[...]
    beyond = [jnp.where(masks[tile], coef_halo[tile], 0.0) for tile in range(tile_count)]
    spread = differences(here) - sum(beyond)
    faces = [jnp.where(masks[tile], here + beyond[tile], 0.0) for tile in range(tile_count)]
    diagonal = terms * DEGREES + 1

    def put(place, k, weight):
        for j, value in enumerate((here, *faces, spread)):
            ctab[place, j] = weight * value[k]

    zero = jnp.zeros((lines, lanes), jnp.float32)
    for j in range(tile_count + 2):
        ctab[0, j] = zero
    for k in range(terms):
        for d in range(DEGREES):
            degree = jnp.full((1, 1), d, jnp.float32)
            weight = (degree + 1.0) * lax.rsqrt((2.0 * degree + 1.0) * (2.0 * degree + 3.0))
            put(k * DEGREES + d + 1, k + 1, 0.5 * weight)
    put(diagonal, 0, 0.5)

    def arrived(source):
        send_z(source)
        block = pl.ds(source * own, own)
        held[block, 1] = differences(held[block, 0])

    own_copy().wait()
    arrived(me)

    @pl.loop(0, n - 1)
    def _(i):
        block_arrived(i)
        arrived(partner(me, i, n, -1))

    for side in (0, 1):
        y_each(side, side, my_slots, lambda copy: copy.start())
    if split:
        for h in (0, 1):
            @pl.when((my_half == h) & (me != edges[h]))
            def _():
                home_copy(h, me).start()

            @pl.when(me == edges[h])
            def _():
                home_own(h).start()

    def main_terms(slot, place):
        value, c = held[slot, 0], ctab[place, 0]
        return [c * value, c * held[slot, 1] - ctab[place, tile_count + 1] * value]

    def outer_terms(some):
        halo = y_halo if some is y_tiles else z_halo
        return lambda slot, place: [ctab[place, 1 + t] * halo[slot, t - some[0]] for t in some]

    def both_terms(slot, place):
        return main_terms(slot, place) + outer_terms(z_tiles)(slot, place)

    def unpacked(table, i, count):
        words = [table[i, j] for j in range((count + 1) // 2)]
        return [part for word in words
                for part in (word & 65535, lax.shift_right_logical(word, 16))][:count]

    def summed(term_of, slot, codes_of):
        total = term_of(slot, diagonal)
        for code in codes_of:
            new = term_of(lax.shift_right_logical(code, 7), code & (CODE - 1))
            total = [a + b for a, b in zip(total, new)]
        return total

    def inner(totals):
        product, other = (jnp.stack(part) for part in zip(*(total[:2] for total in totals)))
        result = differences(product) + other
        return [result[u] for u in range(len(totals))]

    def outer(total, some):
        return sum(jnp.where(masks[t][0], part, 0.0) for t, part in zip(some, total))

    def low_group(stage, first, count, ups, downs):
        term_of = (main_terms, outer_terms(z_tiles), outer_terms(y_tiles))[stage]
        totals = [summed(term_of, slots[first + u],
                         unpacked(up, first + u, ups) + unpacked(down, first + u, downs))
                  for u in range(count)]
        if stage == 0:
            result = inner(totals)
        else:
            result = [outer(total, z_tiles if stage == 1 else y_tiles) for total in totals]
        if stage == 1:
            result = [low_out[0, first + u] - result[u] for u in range(count)]
        for u in range(count):
            low_out[stage // 2, first + u] = result[u]

    def level(stage, first, stop, downs, unroll):
        whole = (stop - first) // unroll

        @pl.loop(0, whole)
        def _(b):
            low_group(stage, first + b * unroll, unroll, terms, downs)

        if first + whole * unroll < stop:
            low_group(stage, first + whole * unroll, stop - first - whole * unroll, terms, downs)

    def all_low(stage):
        level(stage, 0, 1, 0, 1)
        level(stage, 1, linear, 1, UNROLL_LOW)
        level(stage, linear, square, 2, UNROLL_LOW)

    def slot_group(stage, first, count):
        term_of = (both_terms, outer_terms(y_tiles))[stage]
        words = [unpacked(high, first + u, DEGREES + 1) for u in range(count)]
        totals = [summed(term_of, first + u, words[u][:DEGREES]) for u in range(count)]
        if stage == 0:
            result = [a - outer(total[2:], z_tiles) for a, total in zip(inner(totals), totals)]
        else:
            result = [outer(total, y_tiles) for total in totals]
        result = [jnp.where((word[DEGREES] & 1) > 0, result[u], low_out[stage, lax.shift_right_logical(word[DEGREES], 1)])
                  for u, word in enumerate(words)]
        if stage == 1:
            result = [outs[0, first + u] - result[u] for u in range(count)]
        for u in range(count):
            outs[stage, first + u] = result[u]

    def owner(stage, target):
        unroll = max(u for u in range(1, UNROLL_HIGH + 1) if own % u == 0)

        @pl.loop(0, own // unroll)
        def _(b):
            slot_group(stage, target * own + b * unroll, unroll)

    if rows > 2:
        spans = ((pl.ds(depth, lines - 2 * depth),), (pl.ds(0, depth), pl.ds(last, depth)))
    else:
        spans = ((), (pl.ds(0, lines),))

    def back_copies(stage, i, leaving):
        target, source = partner(me, i, n, 1), partner(me, i, n, -1)
        held_by, block = (target, rank) if leaving else (me, rank_of(source, n))
        first = stage * len(spans[0])
        return [pltpu.make_async_remote_copy(
            src_ref=outs.at[stage, pl.ds(held_by * own, own), span], dst_ref=out.at[:, block, span],
            send_sem=back_send.at[first + j, i], recv_sem=back_recv.at[first + j, i],
            device_id=(target, layer), device_id_type=MESH) for j, span in enumerate(spans[stage])]

    def own_back(stage):
        first = stage * len(spans[0])
        return [pltpu.make_async_copy(
            outs.at[stage, pl.ds(me * own, own), span], out.at[:, rank, span], own_sem.at[1 + first + j])
            for j, span in enumerate(spans[stage])]

    for move in moves:
        move.wait()
    for stage in range(2):
        low_out[stage, square] = zero
    all_low(0)
    for side in (2, 3):
        @pl.when(has[source_side[side]])
        def _():
            @pl.loop(0, n)
            def _(source):
                for copy in z_copies(side, source):
                    copy.wait_recv()
    all_low(1)

    for stage in range(2):
        if stage == 1:
            for side in (0, 1):
                y_each(side, source_side[side], other_slots, lambda copy: copy.wait_recv())
            if split:
                for h in (0, 1):
                    @pl.when(me == edges[h])
                    def _():
                        home_own(h).wait()

                        @pl.loop(1, half)
                        def _(j):
                            home_copy(h, h * half + lax.rem(me - h * half + j, half)).wait_recv()
            all_low(2)

        @pl.loop(0, n - 1)
        def _(i):
            owner(stage, partner(me, i, n, 1))
            for copy in back_copies(stage, i, True):
                copy.start()

        owner(stage, me)
        for copy in own_back(stage):
            copy.start()

    @pl.loop(0, n - 1)
    def _(i):
        block_copy(i).wait_send()

    for side in (2, 3):
        @pl.when(has[side])
        def _():
            @pl.loop(0, n)
            def _(source):
                for copy in z_copies(side, source):
                    copy.wait_send()
    for side in (0, 1):
        y_each(side, side, my_slots, lambda copy: copy.wait_send())
    if split:
        for h in (0, 1):
            @pl.when((my_half == h) & (me != edges[h]))
            def _():
                home_copy(h, me).wait_send()
    for stage in range(2):
        for copy in own_back(stage):
            copy.wait()

        @pl.loop(0, n - 1)
        def _(i):
            for copy in back_copies(stage, i, False):
                copy.wait_recv()
            for copy in back_copies(stage, i, True):
                copy.wait_send()


def store_kernel(source, out, held, into, back):
    count = source.shape[0]
    for i in range(count):
        pltpu.make_async_copy(source.at[i], held.at[i], into.at[i]).start()
    for i in range(count):
        pltpu.make_async_copy(source.at[i], held.at[i], into.at[i]).wait()
        pltpu.make_async_copy(held.at[i], out.at[i], back.at[i]).start()
    for i in range(count):
        pltpu.make_async_copy(held.at[i], out.at[i], back.at[i]).wait()


def body(fields, mean_coeff, random_coeff, coupling, mode_slots):
    n, g = lax.axis_size("modes"), lax.axis_size("gz")
    own, row_total, depth, across = fields.shape
    rows = row_total // n
    lines = rows * depth
    terms = random_coeff.shape[0]
    modes, pairs = mode_slots.shape[0], coupling.shape[0]
    f32, i32 = jnp.float32, jnp.int32
    smem = pl.BlockSpec(memory_space=pltpu.SMEM)
    anywhere = pl.BlockSpec(memory_space=pl.ANY)
    dma = pltpu.SemaphoreType.DMA
    tiles, tile_count = side_tiles(rows, depth)
    y_count = tiles[2]
    places = terms * DEGREES + 2
    low_modes = 1 + terms + terms * (terms + 1) // 2
    low_rows = -(-low_modes // 8) * 8
    slot_rows = -(-n * own // 8) * 8

    def tile(*lead):
        return pltpu.VMEM((*lead, lines, across), f32)

    local = (own, n, lines, across)
    operator = pl.pallas_call(
        functools.partial(operator_kernel, n, g, rows, depth, modes, terms),
        out_shape=jax.ShapeDtypeStruct(local, f32),
        in_specs=[smem] + [anywhere] * 4,
        out_specs=anywhere,
        scratch_shapes=[
            tile(n * own, 2), tile(n * own, y_count), tile(n * own, tile_count - y_count),
            tile(2, low_modes + 1), tile(2, n * own),
            pltpu.VMEM((4, pairs), i32), pltpu.VMEM((2, pairs), i32),
            tile(terms + 1), tile(tile_count, terms + 1), tile(places, tile_count + 2),
            *(pltpu.VMEM((size, across), i32) for size in (low_rows, low_rows, slot_rows)),
            *(pltpu.SMEM((size, across), i32) for size in (low_rows, low_rows, slot_rows)),
            dma((4,)), dma((n - 1,)), dma((n - 1,)), dma((3, n - 1)), dma((3, n - 1)),
            dma((2,)), dma((n,)), dma((2,)), dma((2,)), dma((2, n, rows)), dma((2, n, rows)), dma((2, rows, 2)), dma((2, rows, 2)),
            dma((7,)), dma((3,)),
        ],
        compiler_params=pltpu.CompilerParams(collective_id=0, has_side_effects=True),
        name="operator",
    )
    result = operator(
        mode_slots, fields.reshape(local), mean_coeff.reshape(1, n, lines, across),
        random_coeff.reshape(terms, n, lines, across), coupling.T)

    store = pl.pallas_call(
        store_kernel,
        out_shape=jax.ShapeDtypeStruct(local, f32),
        in_specs=[anywhere],
        out_specs=anywhere,
        scratch_shapes=[pltpu.VMEM(local, f32), dma((own,)), dma((own,))],
        name="store",
    )
    return store(result).reshape(fields.shape)


def solution(mesh):
    in_specs = (
        P("modes", None, "gz", None),
        P(None, "gz", None),
        P(None, None, "gz", None),
        P(),
        P(),
    )
    out_specs = P("modes", None, "gz", None)
    return jax.shard_map(body, mesh=mesh, in_specs=in_specs, out_specs=out_specs, check_vma=False)
```

```python
import functools

import jax
import jax.numpy as jnp
from jax import lax
from jax.experimental import pallas as pl
from jax.experimental.pallas import tpu as pltpu
from jax.sharding import PartitionSpec as P

CODE = 128
DEGREES = 3
UNROLL_LOW = 5
UNROLL_HIGH = 9
MESH = pl.DeviceIdType.MESH


def rank_of(index, n):
    if n % 4:
        return index
    a, q = index // 4, lax.rem(index, 4)
    p = q + (q // 2) * (1 - 2 * lax.rem(q, 2))
    return a * 4 + p + lax.rem(a, 2) * (3 - 2 * p)


def index_of(rank, n):
    if n % 4:
        return rank
    a, p = rank // 4, lax.rem(rank, 4)
    p = p + lax.rem(a, 2) * (3 - 2 * p)
    return a * 4 + p + (p // 2) * (1 - 2 * lax.rem(p, 2))


def partner(me, i, n, sign):
    if n & (n - 1):
        return lax.rem(me + sign * (i + 1) + n, n)
    odd = lax.rem(i, 2)
    step = (1 - odd) * (n - 1 - i // 2) + odd * (n // 2 - (i + 1) // 2)
    bit = 1
    other = me
    while bit < n:
        other = other + bit * lax.rem(step // bit, 2) * (1 - 2 * lax.rem(me // bit, 2))
        bit *= 2
    return other


def side_tiles(rows, depth):
    y_high = 0 if rows > 1 else 1
    z_low = y_high + 1
    z_high = z_low if depth > 1 else z_low + 1
    return (0, y_high, z_low, z_high), z_high + 1


def operator_kernel(n, g, rows, depth, modes, terms, slots, fields, mean, random, couple_in,
                    out, held, y_halo, z_halo, low_out, outs, couple, codes, coef, coef_halo, ctab,
                    up_v, down_v, high_v, up, down, high, own_sem, send_sem, recv_sem, back_send,
                    back_recv, home_send, home_recv, ysend, yrecv, zsend, zrecv, csend, crecv, csem, tsem):
    me, layer = lax.axis_index("modes"), lax.axis_index("gz")
    own, lines = fields.shape[0], rows * depth
    lanes = fields.shape[3]
    rank = rank_of(me, n)
    before = index_of(lax.max(rank - 1, 0), n)
    after = index_of(lax.min(rank + 1, n - 1), n)
    tiles, tile_count = side_tiles(rows, depth)
    has = (rank > 0, rank < n - 1, layer > 0, layer < g - 1)
    to = ((before, layer), (after, layer), (me, layer - 1), (me, layer + 1))
    last = (rows - 1) * depth

    def pieces(side, first, count):
        return (
            [(0, depth, tiles[1], last)],
            [(last, depth, tiles[0], 0)],
            [((first + r) * depth, 1, tiles[3], (first + r) * depth + depth - 1) for r in range(count)],
            [((first + r) * depth + depth - 1, 1, tiles[2], (first + r) * depth) for r in range(count)],
        )[side]

    source_side = (1, 0, 3, 2)
    y_tiles, z_tiles = sorted(set(tiles[:2])), sorted(set(tiles[2:]))

    barrier = pltpu.get_barrier_semaphore()

    @pl.loop(1, n)
    def _(step):
        pl.semaphore_signal(barrier, inc=1, device_id=(lax.rem(me + step, n), layer),
                            device_id_type=MESH)

    @pl.loop(1, g)
    def _(step):
        pl.semaphore_signal(barrier, inc=1, device_id=(me, lax.rem(layer + step, g)),
                            device_id_type=MESH)

    pl.semaphore_wait(barrier, n + g - 2)

    def block_copy(i):
        target = partner(me, i, n, 1)
        return pltpu.make_async_remote_copy(
            src_ref=fields.at[:, rank_of(target, n)], dst_ref=held.at[pl.ds(me * own, own), 0],
            send_sem=send_sem.at[i], recv_sem=recv_sem.at[i],
            device_id=(target, layer), device_id_type=MESH)

    def block_arrived(i):
        source = partner(me, i, n, -1)
        pltpu.make_async_remote_copy(
            src_ref=fields.at[:, rank], dst_ref=held.at[pl.ds(source * own, own), 0],
            send_sem=send_sem.at[i], recv_sem=recv_sem.at[i],
            device_id=(source, layer), device_id_type=MESH).wait_recv()

    def own_copy():
        return pltpu.make_async_copy(
            fields.at[:, rank], held.at[pl.ds(me * own, own), 0], own_sem.at[0])

    def y_copy(side, block):
        (line, count, tile, land), = pieces(side, 0, rows)
        return pltpu.make_async_remote_copy(
            src_ref=held.at[block, 0, pl.ds(line, count)], dst_ref=y_halo.at[block, tile, pl.ds(land, count)],
            send_sem=ysend.at[side], recv_sem=yrecv.at[side], device_id=to[side], device_id_type=MESH)

    half = n // 2
    my_half = me // half
    everything, my_slots = pl.ds(0, n * own), pl.ds(my_half * half * own, half * own)
    other_slots = pl.ds((1 - my_half) * half * own, half * own)
    split = n % 8 == 0
    middle = (rank == half, rank == half - 1)
    edges = (index_of(half - 1, n), index_of(half, n))

    def y_each(side, cross_side, slots_there, act):
        if not split:
            @pl.when(has[cross_side])
            def _():
                act(y_copy(side, everything))
            return

        @pl.when(has[cross_side] & jnp.logical_not(middle[cross_side]))
        def _():
            act(y_copy(side, everything))

        @pl.when(middle[cross_side])
        def _():
            act(y_copy(side, slots_there))

    def home_row(h):
        (line, count, tile, land), = pieces(h, 0, rows)
        return (half if h == 0 else half - 1), pl.ds(line, count), tile, pl.ds(land, count)

    def home_copy(h, source):
        block, span, tile, land = home_row(h)
        return pltpu.make_async_remote_copy(
            src_ref=fields.at[:, block, span], dst_ref=y_halo.at[pl.ds(source * own, own), tile, land],
            send_sem=home_send.at[0], recv_sem=home_recv.at[source - h * half],
            device_id=(edges[h], layer), device_id_type=MESH)

    def home_own(h):
        block, span, tile, land = home_row(h)
        return pltpu.make_async_copy(
            fields.at[:, block, span], y_halo.at[pl.ds(me * own, own), tile, land], home_send.at[1])

    def z_copies(side, source):
        block = pl.ds(source * own, own)
        return [pltpu.make_async_remote_copy(
            src_ref=held.at[block, 0, pl.ds(line, count)],
            dst_ref=z_halo.at[block, tile - z_tiles[0], pl.ds(land, count)],
            send_sem=zsend.at[side - 2, source, j], recv_sem=zrecv.at[side - 2, source, j],
            device_id=to[side], device_id_type=MESH)
            for j, (line, count, tile, land) in enumerate(pieces(side, 0, rows))]

    def coef_copies(side):
        copies = []
        for j, (line, count, tile, land) in enumerate(pieces(side, 0, rows)):
            for part, (src, dst) in enumerate((
                    (mean.at[:, rank, pl.ds(line, count)], coef_halo.at[tile, pl.ds(0, 1), pl.ds(land, count)]),
                    (random.at[:, rank, pl.ds(line, count)], coef_halo.at[tile, pl.ds(1, terms), pl.ds(land, count)]))):
                copies.append(pltpu.make_async_remote_copy(
                    src_ref=src, dst_ref=dst, send_sem=csend.at[side - 2, j, part],
                    recv_sem=crecv.at[side - 2, j, part], device_id=to[side], device_id_type=MESH))
        return copies

    @pl.loop(0, n - 1)
    def _(i):
        block_copy(i).start()

    own_copy().start()
    local = [
        pltpu.make_async_copy(couple_in, couple, csem.at[0]),
        pltpu.make_async_copy(mean.at[:, rank], coef.at[pl.ds(0, 1)], csem.at[1]),
        pltpu.make_async_copy(random.at[:, rank], coef.at[pl.ds(1, terms)], csem.at[2]),
    ]
    for copy in local:
        copy.start()

    def row_copies(side):
        line, count, tile, land = pieces(source_side[side], 0, rows)[0]
        there = lax.max(rank - 1, 0) if side == 0 else lax.min(rank + 1, n - 1)
        return [
            pltpu.make_async_copy(mean.at[:, there, pl.ds(line, count)],
                                  coef_halo.at[tile, pl.ds(0, 1), pl.ds(land, count)], csem.at[3 + side]),
            pltpu.make_async_copy(random.at[:, there, pl.ds(line, count)],
                                  coef_halo.at[tile, pl.ds(1, terms), pl.ds(land, count)], csem.at[5 + side])]

    for side in (0, 1):
        @pl.when(has[side])
        def _():
            for copy in row_copies(side):
                copy.start()
    for side in (2, 3):
        @pl.when(has[side])
        def _():
            for copy in coef_copies(side):
                copy.start()

    def send_z(source):
        for side in (2, 3):
            @pl.when(has[side])
            def _():
                for copy in z_copies(side, source):
                    copy.start()

    local[0].wait()
    sub = lax.broadcasted_iota(jnp.int32, (8, lanes), 0)
    lane8 = lax.broadcasted_iota(jnp.int32, (8, lanes), 1)
    pairs = couple.shape[1]
    highest = (n * own - 1) * CODE + terms * DEGREES
    linear = 1 + terms
    square = linear + terms * (terms + 1) // 2

    def slot_block(b, total):
        mode = b * 8 + sub[:, :1]
        slot = jnp.zeros((8, 1), jnp.int32)
        for r in range(8):
            slot = jnp.where(sub[:, :1] == r, slots[jnp.minimum(b * 8 + r, modes - 1)], slot)
        return tuple(t + jnp.where(couple[j:j + 1, :] == mode, slot, 0) for j, t in enumerate(total))

    zeros = jnp.zeros((8, pairs), jnp.int32)
    found = lax.fori_loop(0, -(-modes // 8), slot_block, (zeros, zeros))
    target_slot, source_slot = (jnp.sum(f, axis=0, keepdims=True) for f in found)
    term = couple[2:3, :]
    index = jnp.where(term > 0, (term - 1) * DEGREES + couple[3:4, :] + 1, 0)
    codes[0:1, :] = source_slot * CODE + index
    codes[1:2, :] = target_slot

    def block_of(b):
        return b * 8 + lax.broadcasted_iota(jnp.int32, (8, 1), 0)

    def write(ref, b, values):
        table = jnp.zeros((8, lanes), jnp.int32)
        for k, value in enumerate(values):
            table = jnp.where(lane8 == k, value, table)
        ref[pl.ds(pl.multiple_of(b * 8, 8), 8), :] = jnp.clip(table, 0, highest)

    def lower(mask):
        code, big = codes[0:1, :], 2 ** 23
        mask = mask & (couple[1:2, :] < couple[0:1, :])
        low = jnp.min(jnp.where(mask, code, big), axis=1, keepdims=True)
        high = jnp.max(jnp.where(mask, code, -1), axis=1, keepdims=True)
        total = jnp.sum(jnp.where(mask, code, 0), axis=1, keepdims=True)
        middle = jnp.maximum(total - low - high, 0)
        return [jnp.where(low < big, low, 0), jnp.where(high > low, high, 0), middle]

    @pl.loop(0, up_v.shape[0] // 8)
    def _(b):
        here = couple[0:1, :] == block_of(b)
        code = jnp.where(here & (couple[1:2, :] > couple[0:1, :]), codes[0:1, :], 0)
        write(up_v, b, [jnp.sum(jnp.where(couple[2:3, :] == k + 1, code, 0), axis=1, keepdims=True)
                        for k in range(terms)])
        write(down_v, b, lower(here))

    @pl.loop(0, high_v.shape[0] // 8)
    def _(b):
        here = codes[1:2, :] == block_of(b)
        mode = jnp.where(here & (couple[2:3, :] == 0), couple[0:1, :] - modes, 0)
        mode = jnp.sum(mode, axis=1, keepdims=True) + modes
        is_high = (mode >= square) & (mode < modes)
        write(high_v, b, lower(here) + [jnp.clip(mode, 0, square), jnp.where(is_high, 1, 0)])

    moves = [pltpu.make_async_copy(a, b, tsem.at[i])
             for i, (a, b) in enumerate(((up_v, up), (down_v, down), (high_v, high)))]
    for move in moves:
        move.start()

    line = lax.broadcasted_iota(jnp.int32, (1, lines, lanes), 1)
    lane = lax.broadcasted_iota(jnp.int32, (1, lines, lanes), 2)
    row, deep = line // depth, lax.rem(line, depth)
    side_masks = (
        (row == 0) & has[0], (row == rows - 1) & has[1],
        (deep == 0) & has[2], (deep == depth - 1) & has[3],
    )

    def differences(value):
        total = 6.0 * value
        if rows > 1:
            total -= jnp.where(row == 0, 0.0, pltpu.roll(value, depth, 1))
            total -= jnp.where(row == rows - 1, 0.0, pltpu.roll(value, lines - depth, 1))
        if depth > 1:
            up_one, down_one = pltpu.roll(value, 1, 1), pltpu.roll(value, lines - 1, 1)
            if depth == 2:
                total -= jnp.where(deep == 0, down_one, up_one)
            else:
                total -= jnp.where(deep == 0, 0.0, up_one) + jnp.where(deep == depth - 1, 0.0, down_one)
        total -= jnp.where(lane == 0, 0.0, pltpu.roll(value, 1, 2))
        total -= jnp.where(lane == lanes - 1, 0.0, pltpu.roll(value, lanes - 1, 2))
        return total

    masks = []
    for tile in range(tile_count):
        sides = [side_masks[side] for side in range(4) if tiles[side] == tile]
        masks.append(functools.reduce(jnp.logical_or, sides))

    for copy in local[1:]:
        copy.wait()
    for side in (0, 1):
        @pl.when(has[side])
        def _():
            for copy in row_copies(side):
                copy.wait()
    for side in (2, 3):
        @pl.when(has[side])
        def _():
            for copy in coef_copies(side):
                copy.wait_send()

        @pl.when(has[source_side[side]])
        def _():
            for copy in coef_copies(side):
                copy.wait_recv()

    here = coef[...]
    beyond = [jnp.where(masks[tile], coef_halo[tile], 0.0) for tile in range(tile_count)]
    spread = differences(here) - sum(beyond)
    faces = [jnp.where(masks[tile], here + beyond[tile], 0.0) for tile in range(tile_count)]
    diagonal = terms * DEGREES + 1

    def put(place, k, weight):
        for j, value in enumerate((here, *faces, spread)):
            ctab[place, j] = weight * value[k]

    zero = jnp.zeros((lines, lanes), jnp.float32)
    for j in range(tile_count + 2):
        ctab[0, j] = zero
    for k in range(terms):
        for d in range(DEGREES):
            degree = jnp.full((1, 1), d, jnp.float32)
            weight = (degree + 1.0) * lax.rsqrt((2.0 * degree + 1.0) * (2.0 * degree + 3.0))
            put(k * DEGREES + d + 1, k + 1, 0.5 * weight)
    put(diagonal, 0, 0.5)

    def arrived(source):
        send_z(source)
        block = pl.ds(source * own, own)
        held[block, 1] = differences(held[block, 0])

    own_copy().wait()
    arrived(me)

    @pl.loop(0, n - 1)
    def _(i):
        block_arrived(i)
        arrived(partner(me, i, n, -1))

    for side in (0, 1):
        y_each(side, side, my_slots, lambda copy: copy.start())
    if split:
        for h in (0, 1):
            @pl.when((my_half == h) & (me != edges[h]))
            def _():
                home_copy(h, me).start()

            @pl.when(me == edges[h])
            def _():
                home_own(h).start()

    def main_terms(slot, place):
        value, c = held[slot, 0], ctab[place, 0]
        return [c * value, c * held[slot, 1] - ctab[place, tile_count + 1] * value]

    def outer_terms(some):
        halo = y_halo if some is y_tiles else z_halo
        return lambda slot, place: [ctab[place, 1 + t] * halo[slot, t - some[0]] for t in some]

    def both_terms(slot, place):
        return main_terms(slot, place) + outer_terms(z_tiles)(slot, place)

    def summed(term_of, slot, codes_of):
        total = term_of(slot, diagonal)
        for code in codes_of:
            new = term_of(lax.shift_right_logical(code, 7), code & (CODE - 1))
            total = [a + b for a, b in zip(total, new)]
        return total

    def inner(totals):
        product, other = (jnp.stack(part) for part in zip(*(total[:2] for total in totals)))
        result = differences(product) + other
        return [result[u] for u in range(len(totals))]

    def outer(total, some):
        return sum(jnp.where(masks[t][0], part, 0.0) for t, part in zip(some, total))

    def low_group(stage, first, count, ups, downs):
        term_of = (main_terms, outer_terms(z_tiles), outer_terms(y_tiles))[stage]
        totals = [summed(term_of, slots[first + u],
                         [up[first + u, k] for k in range(ups)] + [down[first + u, k] for k in range(downs)])
                  for u in range(count)]
        if stage == 0:
            result = inner(totals)
        else:
            result = [outer(total, z_tiles if stage == 1 else y_tiles) for total in totals]
        if stage == 1:
            result = [low_out[0, first + u] - result[u] for u in range(count)]
        for u in range(count):
            low_out[stage // 2, first + u] = result[u]

    def level(stage, first, stop, downs, unroll):
        whole = (stop - first) // unroll

        @pl.loop(0, whole)
        def _(b):
            low_group(stage, first + b * unroll, unroll, terms, downs)

        if first + whole * unroll < stop:
            low_group(stage, first + whole * unroll, stop - first - whole * unroll, terms, downs)

    def all_low(stage):
        level(stage, 0, 1, 0, 1)
        level(stage, 1, linear, 1, UNROLL_LOW)
        level(stage, linear, square, 2, UNROLL_LOW)

    def slot_group(stage, first, count):
        term_of = (both_terms, outer_terms(y_tiles))[stage]
        totals = [summed(term_of, first + u, [high[first + u, k] for k in range(DEGREES)])
                  for u in range(count)]
        if stage == 0:
            result = [a - outer(total[2:], z_tiles) for a, total in zip(inner(totals), totals)]
        else:
            result = [outer(total, y_tiles) for total in totals]
        result = [jnp.where(high[first + u, 4] > 0, result[u], low_out[stage, high[first + u, 3]])
                  for u in range(count)]
        if stage == 1:
            result = [outs[0, first + u] - result[u] for u in range(count)]
        for u in range(count):
            outs[stage, first + u] = result[u]

    def owner(stage, target):
        unroll = max(u for u in range(1, UNROLL_HIGH + 1) if own % u == 0)

        @pl.loop(0, own // unroll)
        def _(b):
            slot_group(stage, target * own + b * unroll, unroll)

    if rows > 2:
        spans = ((pl.ds(depth, lines - 2 * depth),), (pl.ds(0, depth), pl.ds(last, depth)))
    else:
        spans = ((), (pl.ds(0, lines),))

    def back_copies(stage, i, leaving):
        target, source = partner(me, i, n, 1), partner(me, i, n, -1)
        held_by, block = (target, rank) if leaving else (me, rank_of(source, n))
        first = stage * len(spans[0])
        return [pltpu.make_async_remote_copy(
            src_ref=outs.at[stage, pl.ds(held_by * own, own), span], dst_ref=out.at[:, block, span],
            send_sem=back_send.at[first + j, i], recv_sem=back_recv.at[first + j, i],
            device_id=(target, layer), device_id_type=MESH) for j, span in enumerate(spans[stage])]

    def own_back(stage):
        first = stage * len(spans[0])
        return [pltpu.make_async_copy(
            outs.at[stage, pl.ds(me * own, own), span], out.at[:, rank, span], own_sem.at[1 + first + j])
            for j, span in enumerate(spans[stage])]

    for move in moves:
        move.wait()
    for stage in range(2):
        low_out[stage, square] = zero
    all_low(0)
    for side in (2, 3):
        @pl.when(has[source_side[side]])
        def _():
            @pl.loop(0, n)
            def _(source):
                for copy in z_copies(side, source):
                    copy.wait_recv()
    all_low(1)

    for stage in range(2):
        if stage == 1:
            for side in (0, 1):
                y_each(side, source_side[side], other_slots, lambda copy: copy.wait_recv())
            if split:
                for h in (0, 1):
                    @pl.when(me == edges[h])
                    def _():
                        home_own(h).wait()

                        @pl.loop(1, half)
                        def _(j):
                            home_copy(h, h * half + lax.rem(me - h * half + j, half)).wait_recv()
            all_low(2)

        @pl.loop(0, n - 1)
        def _(i):
            owner(stage, partner(me, i, n, 1))
            for copy in back_copies(stage, i, True):
                copy.start()

        owner(stage, me)
        for copy in own_back(stage):
            copy.start()

    @pl.loop(0, n - 1)
    def _(i):
        block_copy(i).wait_send()

    for side in (2, 3):
        @pl.when(has[side])
        def _():
            @pl.loop(0, n)
            def _(source):
                for copy in z_copies(side, source):
                    copy.wait_send()
    for side in (0, 1):
        y_each(side, side, my_slots, lambda copy: copy.wait_send())
    if split:
        for h in (0, 1):
            @pl.when((my_half == h) & (me != edges[h]))
            def _():
                home_copy(h, me).wait_send()
    for stage in range(2):
        for copy in own_back(stage):
            copy.wait()

        @pl.loop(0, n - 1)
        def _(i):
            for copy in back_copies(stage, i, False):
                copy.wait_recv()
            for copy in back_copies(stage, i, True):
                copy.wait_send()


def store_kernel(source, out, held, into, back):
    count = source.shape[0]
    per = 3 if count % 3 == 0 else 1
    parts = [pl.ds(i, per) for i in range(0, count, per)]
    for i, part in enumerate(parts):
        pltpu.make_async_copy(source.at[part], held.at[part], into.at[i]).start()
    for i, part in enumerate(parts):
        pltpu.make_async_copy(source.at[part], held.at[part], into.at[i]).wait()
        pltpu.make_async_copy(held.at[part], out.at[part], back.at[i]).start()
    for i, part in enumerate(parts):
        pltpu.make_async_copy(held.at[part], out.at[part], back.at[i]).wait()


def body(fields, mean_coeff, random_coeff, coupling, mode_slots):
    n, g = lax.axis_size("modes"), lax.axis_size("gz")
    own, row_total, depth, across = fields.shape
    rows = row_total // n
    lines = rows * depth
    terms = random_coeff.shape[0]
    modes, pairs = mode_slots.shape[0], coupling.shape[0]
    f32, i32 = jnp.float32, jnp.int32
    smem = pl.BlockSpec(memory_space=pltpu.SMEM)
    anywhere = pl.BlockSpec(memory_space=pl.ANY)
    dma = pltpu.SemaphoreType.DMA
    tiles, tile_count = side_tiles(rows, depth)
    y_count = tiles[2]
    places = terms * DEGREES + 2
    low_modes = 1 + terms + terms * (terms + 1) // 2
    low_rows = -(-low_modes // 8) * 8
    slot_rows = -(-n * own // 8) * 8

    def tile(*lead):
        return pltpu.VMEM((*lead, lines, across), f32)

    local = (own, n, lines, across)
    operator = pl.pallas_call(
        functools.partial(operator_kernel, n, g, rows, depth, modes, terms),
        out_shape=jax.ShapeDtypeStruct(local, f32),
        in_specs=[smem] + [anywhere] * 4,
        out_specs=anywhere,
        scratch_shapes=[
            tile(n * own, 2), tile(n * own, y_count), tile(n * own, tile_count - y_count),
            tile(2, low_modes + 1), tile(2, n * own),
            pltpu.VMEM((4, pairs), i32), pltpu.VMEM((2, pairs), i32),
            tile(terms + 1), tile(tile_count, terms + 1), tile(places, tile_count + 2),
            *(pltpu.VMEM((size, across), i32) for size in (low_rows, low_rows, slot_rows)),
            *(pltpu.SMEM((size, across), i32) for size in (low_rows, low_rows, slot_rows)),
            dma((4,)), dma((n - 1,)), dma((n - 1,)), dma((3, n - 1)), dma((3, n - 1)),
            dma((2,)), dma((n,)), dma((2,)), dma((2,)), dma((2, n, rows)), dma((2, n, rows)), dma((2, rows, 2)), dma((2, rows, 2)),
            dma((7,)), dma((3,)),
        ],
        compiler_params=pltpu.CompilerParams(collective_id=0, has_side_effects=True),
        name="operator",
    )
    result = operator(
        mode_slots, fields.reshape(local), mean_coeff.reshape(1, n, lines, across),
        random_coeff.reshape(terms, n, lines, across), coupling.T)

    store = pl.pallas_call(
        store_kernel,
        out_shape=jax.ShapeDtypeStruct(local, f32),
        in_specs=[anywhere],
        out_specs=anywhere,
        scratch_shapes=[pltpu.VMEM(local, f32), dma((own,)), dma((own,))],
        name="store",
    )
    return store(result).reshape(fields.shape)


def solution(mesh):
    in_specs = (
        P("modes", None, "gz", None),
        P(None, "gz", None),
        P(None, None, "gz", None),
        P(),
        P(),
    )
    out_specs = P("modes", None, "gz", None)
    return jax.shard_map(body, mesh=mesh, in_specs=in_specs, out_specs=out_specs, check_vma=False)
```
